32 devices in a mesh: ctx: 8 (over z, core), ch: 4 (over y, x).
Axes of the slice: x: 2, y: 2, z: 4, core: 2. Of those that a mesh axis runs over, the one named last changes fastest.
Arguments:
- features: bfloat16 [3, 2048, 8192], P(None, 'ctx', 'ch'), may hold values from -6 to 6
- short_filter: float32 [3, 7, 8192], P(None, None, 'ch'), may hold values from -4 to 4
- long_filter: float32 [512, 128], P('ch'), may hold values from -0.5 to 0.5
- cotangent: bfloat16 [2048, 8192], P('ctx', 'ch'), may hold values from -15 to 15
Outputs:
- grad_features: bfloat16 [3, 2048, 8192], P(None, 'ctx', 'ch')
- grad_short: float32 [3, 7, 8192], P(None, None, 'ch')
- grad_long: float32 [512, 128], P('ch')
The draws below stay inside these ranges and needn't reach their ends.
All inputs are finite; a program needn't handle non-finite values.
Results may differ from the reference program's by a relative error of at most 0.0057.
Values may be sent and summed in bfloat16 or wider, within the bound.
No kernel may reach another device: no remote copies, remote signals or barrier semaphores. Data moves between devices by JAX's collectives and lax.ppermute only.
A program may use at most 128 MiB of HBM per device.

```python
import math
import jax
import jax.numpy as jnp
from jax import lax

D = 8192
GROUP = 16
G = 512
SHORT_TAPS = 7
LONG_TAPS = 128
TOKENS = 2048


def draw_cotangent(key, part):
    scale_key, value_key = jax.random.split(jax.random.fold_in(key, 11))
    scales = jnp.exp(jax.random.uniform(scale_key, (D,), jnp.float32, math.log(0.5), math.log(5.0)))
    values = jax.random.truncated_normal(value_key, -3.0, 3.0, (TOKENS, D), jnp.float32)
    return (values * scales[None, :]).astype(jnp.bfloat16)


def level_of(key, shape, shards, least, top_value):
    loudness = 1.0
    for position, blocks in shards:
        heights = jax.random.uniform(jax.random.fold_in(jax.random.fold_in(key, 6), position), (blocks,), jnp.float32, least / len(shards), top_value / len(shards))
        loudness = loudness * jnp.repeat(jnp.exp(heights), shape[position] // blocks).reshape((-1,) + (1,) * (len(shape) - 1 - position))
    return loudness


def normal_values(stream_key, shape, width, limit, shards=(), kind=jnp.bfloat16):
    loudness = level_of(stream_key, shape, shards, -0.22, 0.18) if shards else 1.0
    drawn = jax.random.normal(stream_key, shape, jnp.float32) * width * loudness
    return jnp.minimum(jnp.maximum(drawn, -limit), limit).astype(kind)


def setup_inputs(seed: int = 0) -> dict:
    key_of = jax.random.split(jax.random.key(seed), 5)
    return {
        "features": normal_values(key_of[0], (3, TOKENS, D), 1.0, 6.0, ((1, 8), (2, 4))),
        "short_filter": normal_values(key_of[1], (3, SHORT_TAPS, D), 0.4, 4.0, ((2, 4),), jnp.float32),
        "long_filter": normal_values(key_of[2], (G, LONG_TAPS), 0.09, 0.5, ((0, 4),), jnp.float32),
        "cotangent": draw_cotangent(jax.random.fold_in(key_of[4], 71), 0),
    }


def short_conv(extended, filt, count):
    taps = filt.shape[0]
    total = jnp.zeros((count, extended.shape[1]), jnp.float32)
    for tap in range(taps):
        start = taps - 1 - tap
        total = total + filt[tap] * extended[start:start + count].astype(jnp.float32)
    return total

def short_adjoint(grad, filt):
    taps = filt.shape[0]
    count = grad.shape[0]
    edge = jnp.zeros((taps - 1, grad.shape[1]), jnp.float32)
    padded = jnp.concatenate([edge, grad, edge], 0)
    total = jnp.zeros((count + taps - 1, grad.shape[1]), jnp.float32)
    for tap in range(taps):
        total = total + filt[tap] * padded[tap:tap + count + taps - 1]
    return total

def filter_grad(grad, extended, taps):
    count = grad.shape[0]
    pieces = []
    for tap in range(taps):
        start = taps - 1 - tap
        pieces.append(lax.optimization_barrier(jnp.sum(grad * extended[start:start + count].astype(jnp.float32), 0)))
    return jnp.stack(pieces)

def toeplitz(long_filter):
    groups, span = long_filter.shape
    rounded = long_filter.astype(jnp.bfloat16).astype(jnp.float32)
    line = jnp.concatenate([jnp.zeros((groups, 1), jnp.float32), rounded[:, ::-1], jnp.zeros((groups, 2 * span - 1), jnp.float32)], 1)
    flat = jnp.tile(line, (1, span))[:, :span * (3 * span - 1)]
    return flat.reshape(groups, span, 3 * span - 1)[:, :, :2 * span]

def windows(z_pad, groups, span):
    count = z_pad.shape[0] // span
    blocks = z_pad.astype(jnp.float32).reshape(count, span, groups, -1)
    return jnp.concatenate([blocks[:-1], blocks[1:]], 1)

def long_forward(z_pad, matrix, groups, span):
    win = windows(z_pad, groups, span)
    out = jnp.einsum('gts,bsgc->btgc', matrix, win, precision=lax.Precision.HIGHEST)
    return out.reshape(-1, z_pad.shape[1])

def long_adjoint(grad_y, matrix, groups, span):
    count = grad_y.shape[0] // span
    blocks = grad_y.astype(jnp.float32).reshape(count, span, groups, -1)
    win = jnp.einsum('gts,btgc->bsgc', matrix, blocks, precision=lax.Precision.HIGHEST)
    zero = jnp.zeros((1,) + win.shape[1:2] + win.shape[2:], jnp.float32)[:, :span]
    total = jnp.concatenate([win[:, :span], zero], 0) + jnp.concatenate([zero, win[:, span:]], 0)
    return total.reshape(-1, grad_y.shape[1])

def long_filter_grad(grad_y, z_pad, groups, span):
    count = grad_y.shape[0] // span
    blocks = grad_y.astype(jnp.float32).reshape(count, span, groups, -1)
    win = windows(z_pad, groups, span)
    inner = jnp.einsum('btgc,bsgc->gts', blocks, win, precision=lax.Precision.HIGHEST)
    inner = jnp.concatenate([inner, jnp.zeros((groups, span, span), jnp.float32)], 2)
    flat = jnp.concatenate([inner.reshape(groups, span * 3 * span), jnp.zeros((groups, span), jnp.float32)], 1)
    skewed = flat.reshape(groups, span, 3 * span + 1)
    columns = lax.optimization_barrier(jnp.sum(skewed, 1))
    return columns[:, 1:span + 1][:, ::-1]

def reference(features, short_filter, long_filter, cotangent):
    taps = SHORT_TAPS
    span = LONG_TAPS
    reach = span + taps - 2
    block = math.gcd(D, 512)
    count = D // block
    groups = block // GROUP

    def one_block(index):
        first = (index * block).astype(jnp.int32)
        feats = lax.dynamic_slice_in_dim(features, first, block, 2)
        filt = lax.dynamic_slice_in_dim(short_filter, first, block, 2)
        longf = lax.dynamic_slice_in_dim(long_filter, (index * groups).astype(jnp.int32), groups, 0)
        cot = lax.dynamic_slice_in_dim(cotangent, first, block, 1).astype(jnp.float32)
        q_ext = jnp.concatenate([jnp.zeros((taps - 1, block), jnp.bfloat16), feats[0]], 0)
        k_ext = jnp.concatenate([jnp.zeros((reach, block), jnp.bfloat16), feats[1]], 0)
        v_ext = jnp.concatenate([jnp.zeros((reach, block), jnp.bfloat16), feats[2]], 0)
        q_short = short_conv(q_ext, filt[0], TOKENS)
        k_short = short_conv(k_ext, filt[1], TOKENS + span - 1)
        v_short = short_conv(v_ext, filt[2], TOKENS + span - 1)
        gated = (k_short * v_short).astype(jnp.bfloat16)
        z_pad = jnp.concatenate([jnp.zeros((1, block), jnp.bfloat16), gated], 0)
        matrix = toeplitz(longf)
        y_long = long_forward(z_pad, matrix, groups, span)
        grad_y = (cot * q_short).astype(jnp.bfloat16)
        grad_q_short = cot * y_long
        grad_z = long_adjoint(grad_y, matrix, groups, span)[1:]
        grad_k_short = grad_z * v_short
        grad_v_short = grad_z * k_short
        grad_q = short_adjoint(grad_q_short, filt[0])[taps - 1:]
        grad_k = short_adjoint(grad_k_short, filt[1])[reach:]
        grad_v = short_adjoint(grad_v_short, filt[2])[reach:]
        raw_short = jnp.stack([filter_grad(grad_q_short, q_ext, taps), filter_grad(grad_k_short, k_ext, taps), filter_grad(grad_v_short, v_ext, taps)])
        raw_long = long_filter_grad(grad_y, z_pad, groups, span)
        grads = jnp.stack([grad_q, grad_k, grad_v]).astype(jnp.bfloat16)
        return (grads, raw_short, raw_long)
    grads, raw_short, raw_long = lax.map(one_block, jnp.arange(count, dtype=jnp.int32))
    grad_features = grads.transpose(1, 2, 0, 3).reshape(3, TOKENS, D)
    raw_short = raw_short.transpose(1, 2, 0, 3).reshape(3, taps, D)
    raw_long = raw_long.reshape(G, span)
    mean_square = (jnp.sum(raw_short * raw_short) + jnp.sum(raw_long * raw_long)) / (3 * taps * D + span * G)
    factor = lax.rsqrt(mean_square + 1e-06)
    return (grad_features, raw_short * factor, raw_long * factor)
```

```python
import functools

import jax
import jax.numpy as jnp
from jax import lax
from jax.experimental import pallas as pl
from jax.experimental.pallas import tpu as pltpu
from jax.sharding import PartitionSpec as P

D = 8192
G = 512
LANES = 128
EDGE = 8
F32 = jnp.float32
BF16 = jnp.bfloat16


def taps_of(filt, which, lanes):
    return [filt[which, pl.ds(j, 1), lanes] for j in range(filt.shape[1])]


def conv(source, taps, base, count):
    total = None
    for j, tap in enumerate(taps):
        term = tap * source[pl.ds(base - j, count), :]
        total = term if total is None else total + term
    return total


def chunks(count, size):
    return [(at, min(size, count - at)) for at in range(0, count, size)]


def edge_kernel(span, feat, cot, filt, ahead, back, qx, kx, vx):
    rows = feat.shape[1]
    width = feat.shape[2]
    reach = span + 2 * EDGE

    def tile(i, carry):
        lanes = pl.ds(pl.multiple_of(i * LANES, LANES), LANES)
        qx[...] = feat[0, 0:reach, lanes].astype(F32)
        kx[...] = feat[1, rows - reach : rows, lanes].astype(F32)
        vx[...] = feat[2, rows - reach : rows, lanes].astype(F32)
        fq, fk, fv = (taps_of(filt, a, lanes) for a in range(3))
        for at, size in chunks(span, 32):
            z = conv(kx, fk, at + 2 * EDGE, size) * conv(vx, fv, at + 2 * EDGE, size)
            ahead[at : at + size, lanes] = z.astype(BF16)
        q_tail = feat[0, rows - 2 * EDGE : rows, lanes].astype(F32)[EDGE:]
        tails = jnp.concatenate([q_tail, kx[reach - EDGE : reach, :]], 0)
        ahead[span : span + 2 * EDGE, lanes] = tails.astype(BF16)
        ahead[span + 2 * EDGE : span + 3 * EDGE, lanes] = vx[reach - EDGE : reach, :].astype(BF16)
        for at, size in chunks(span + EDGE, 32):
            low = max(at, EDGE)
            c = cot[at : at + max(size, 2 * EDGE), lanes].astype(F32)[low - at : size]
            dy = conv(qx, fq, low, at + size - low) * c
            if at == 0:
                dy = jnp.concatenate([qx[0:EDGE, :], dy], 0)
            back[at : at + size, lanes] = dy.astype(BF16)
        heads = [feat[a, 0 : 2 * EDGE, lanes].astype(F32)[:EDGE] for a in (1, 2)]
        heads.append(cot[0 : 2 * EDGE, lanes].astype(F32)[:EDGE])
        back[span + EDGE : span + 4 * EDGE, lanes] = jnp.concatenate(heads, 0).astype(BF16)
        return carry

    lax.fori_loop(0, width // LANES, tile, 0)


def edges(features, cotangent, short_filter, span):
    _, rows, width = features.shape
    taps = short_filter.shape[1]
    step = min(width, 1024)
    return pl.pallas_call(
        functools.partial(edge_kernel, span),
        grid=(width // step,),
        in_specs=[
            pl.BlockSpec((3, rows, step), lambda i: (0, 0, i)),
            pl.BlockSpec((rows, step), lambda i: (0, i)),
            pl.BlockSpec((3, taps, step), lambda i: (0, 0, i)),
        ],
        out_specs=[
            pl.BlockSpec((span + 3 * EDGE, step), lambda i: (0, i)),
            pl.BlockSpec((span + 4 * EDGE, step), lambda i: (0, i)),
        ],
        out_shape=[
            jax.ShapeDtypeStruct((span + 3 * EDGE, width), BF16),
            jax.ShapeDtypeStruct((span + 4 * EDGE, width), BF16),
        ],
        scratch_shapes=[pltpu.VMEM((span + 2 * EDGE, LANES), F32)] * 3,
        name="edges",
    )(features, cotangent, short_filter)


def dot(a, b, dims=((1,), (0,))):
    return lax.dot_general(a, b, (dims, ((), ())), preferred_element_type=F32)


def main_kernel(
    span, members,
    feat, cot, ahead, back, filt, lines,
    grads, sums,
    qx, kx, vx, ksx, vsx, zx, dyx, dqx, dkx, dvx, tst, ust, zm,
):
    rows = feat.shape[1]
    width = feat.shape[2]
    blocks = rows // span
    wide = rows + EDGE
    per = LANES // members

    @pl.when(pl.program_id(0) == 0)
    def _():
        zx[...] = jnp.zeros_like(zx)
        dyx[...] = jnp.zeros_like(dyx)

    def tile(i, carry):
        lanes = pl.ds(pl.multiple_of(i * LANES, LANES), LANES)
        fq, fk, fv = (taps_of(filt, a, lanes) for a in range(3))
        ends = ahead[span : span + 2 * EDGE, lanes].astype(F32)
        qx[0:EDGE, :] = ends[:EDGE]
        kx[0:EDGE, :] = ends[EDGE:]
        vx[0:EDGE, :] = ahead[span + 2 * EDGE : span + 3 * EDGE, lanes].astype(F32)
        for a, x in enumerate((qx, kx, vx)):
            for at, size in chunks(rows, 32):
                x[EDGE + at : EDGE + at + size, :] = feat[a, at : at + size, lanes].astype(F32)
        first = back[0 : 2 * EDGE, lanes].astype(F32)
        last = back[span + EDGE : span + 4 * EDGE, lanes].astype(F32)
        qx[EDGE + rows : EDGE + wide, :] = first[:EDGE]
        kx[EDGE + rows : EDGE + wide, :] = last[:EDGE]
        vx[EDGE + rows : EDGE + wide, :] = last[EDGE : 2 * EDGE]
        c_next = last[2 * EDGE :]

        zx[0:span, :] = ahead[0:span, lanes]
        for at, size in chunks(wide, 32):
            ks = conv(kx, fk, EDGE + at, size)
            vs = conv(vx, fv, EDGE + at, size)
            ksx[at : at + size, :] = ks
            vsx[at : at + size, :] = vs
            zx[span + at : span + at + size, :] = (ks * vs).astype(BF16)
        for at, size in chunks(rows, 32):
            c = cot[at : at + size, lanes].astype(F32)
            dyx[at : at + size, :] = (c * conv(qx, fq, EDGE + at, size)).astype(BF16)
        dy_next = c_next * conv(qx, fq, EDGE + rows, EDGE)
        dyx[rows : rows + 2 * EDGE, :] = jnp.concatenate([dy_next, first[EDGE:]], 0).astype(BF16)
        dyx[rows + 2 * EDGE : rows + span + EDGE, :] = back[2 * EDGE : span + EDGE, lanes]

        for g in range(per):
            for which, out in ((0, tst), (1, ust)):
                line = lines[which, pl.ds(i * per + g, 1), :]
                spread = jnp.broadcast_to(line, (span, 2 * span))
                turned = pltpu.roll(spread, 0, 1, stride=1, stride_axis=0)
                out[g * span : (g + 1) * span, :] = turned.astype(BF16)

        lane_group = lax.broadcasted_iota(jnp.int32, (1, LANES), 1) // members
        wide_group = jnp.concatenate([lane_group] * blocks, 1)

        def pick(stacked, size, owner):
            total = stacked[0:size]
            for g in range(1, per):
                total = jnp.where(owner == g, stacked[g * size : (g + 1) * size], total)
            return total

        def heads_of(matrix):
            return jnp.concatenate(
                [matrix[g * span : g * span + 2 * EDGE, :] for g in range(per)], 0
            )

        z_win = jnp.concatenate([zx[b * span : (b + 2) * span, :] for b in range(blocks)], 1)
        y = pick(dot(tst[...], z_win), span, wide_group)
        y_next = pick(dot(heads_of(tst), zx[rows : rows + 2 * span, :]), 2 * EDGE, lane_group)
        for b in range(blocks):
            for at, size in chunks(span, 32):
                t = b * span + at
                c = cot[t : t + size, lanes].astype(F32)
                dqx[t : t + size, :] = c * y[at : at + size, b * LANES : (b + 1) * LANES]
        dqx[rows:wide, :] = c_next * y_next[:EDGE]

        d_win = jnp.concatenate([dyx[b * span : (b + 2) * span, :] for b in range(blocks)], 1)
        dz = pick(dot(ust[...], d_win), span, wide_group)
        dz_next = pick(dot(heads_of(ust), dyx[rows : rows + 2 * span, :]), 2 * EDGE, lane_group)
        for b in range(blocks):
            for at, size in chunks(span, 32):
                t = b * span + at
                piece = dz[at : at + size, b * LANES : (b + 1) * LANES]
                dkx[t : t + size, :] = piece * vsx[t : t + size, :]
                dvx[t : t + size, :] = piece * ksx[t : t + size, :]
        dkx[rows:wide, :] = dz_next[:EDGE] * vsx[rows:wide, :]
        dvx[rows:wide, :] = dz_next[:EDGE] * ksx[rows:wide, :]

        r = lax.broadcasted_iota(jnp.int32, (span, span), 0)
        s = lax.broadcasted_iota(jnp.int32, (span, span), 1)
        flip = jnp.where(r + s == span - 1, 1.0, 0.0).astype(BF16)
        z_own = jnp.concatenate([zx[(b + 1) * span : (b + 2) * span, :] for b in range(blocks)], 1)
        z_back = dot(flip, z_own)
        for g in range(per):
            kept = jnp.where(wide_group == g, z_back, 0.0)
            zm[g * span : (g + 1) * span, :] = kept.astype(BF16)
        pairs = dot(zm[...], d_win, ((1,), (1,)))
        for g in range(per):
            part = pltpu.roll(
                pairs[g * span : (g + 1) * span, :], span + 1, 1, stride=1, stride_axis=0
            )
            sums[3 * EDGE + g : 3 * EDGE + g + 1, lanes] = jnp.sum(
                part[:, :span], 0, keepdims=True
            )

        for a, (x, dx, taps) in enumerate(((qx, dqx, fq), (kx, dkx, fk), (vx, dvx, fv))):
            parts = [None] * len(taps)
            for at, size in chunks(rows, 32):
                own = x[EDGE + at : EDGE + at + size, :]
                total = None
                for j, tap in enumerate(taps):
                    moved = dx[pl.ds(at + j, size), :]
                    term = tap * moved
                    total = term if total is None else total + term
                    prod = jnp.sum((own * moved).reshape(size // EDGE, EDGE, LANES), 0)
                    parts[j] = prod if parts[j] is None else parts[j] + prod
                grads[a, at : at + size, lanes] = total.astype(BF16)
            found = [jnp.sum(p, 0, keepdims=True) for p in parts]
            found.append(jnp.zeros((EDGE - len(taps), LANES), F32))
            sums[a * EDGE : (a + 1) * EDGE, lanes] = jnp.concatenate(found, 0)
        return carry

    lax.fori_loop(0, width // LANES, tile, 0)


def main(features, cotangent, ahead, back, short_filter, lines, span, members):
    _, rows, width = features.shape
    taps = short_filter.shape[1]
    step = min(width, 512)
    per = LANES // members
    blocks = rows // span
    wide = rows + EDGE
    tall = (blocks + 2) * span
    return pl.pallas_call(
        functools.partial(main_kernel, span, members),
        grid=(width // step,),
        in_specs=[
            pl.BlockSpec((3, rows, step), lambda i: (0, 0, i)),
            pl.BlockSpec((rows, step), lambda i: (0, i)),
            pl.BlockSpec((span + 3 * EDGE, step), lambda i: (0, i)),
            pl.BlockSpec((span + 4 * EDGE, step), lambda i: (0, i)),
            pl.BlockSpec((3, taps, step), lambda i: (0, 0, i)),
            pl.BlockSpec((2, step // members, 2 * span), lambda i: (0, i, 0)),
        ],
        out_specs=[
            pl.BlockSpec((3, rows, step), lambda i: (0, 0, i)),
            pl.BlockSpec((3 * EDGE + per, step), lambda i: (0, i)),
        ],
        out_shape=[
            jax.ShapeDtypeStruct((3, rows, width), BF16),
            jax.ShapeDtypeStruct((3 * EDGE + per, width), F32),
        ],
        scratch_shapes=[pltpu.VMEM((wide + EDGE, LANES), F32)] * 3
        + [pltpu.VMEM((wide, LANES), F32)] * 2
        + [pltpu.VMEM((tall, LANES), BF16)] * 2
        + [pltpu.VMEM((wide, LANES), F32)] * 3
        + [pltpu.VMEM((per * span, 2 * span), BF16)] * 2
        + [pltpu.VMEM((per * span, blocks * LANES), BF16)],
        compiler_params=pltpu.CompilerParams(vmem_limit_bytes=60 * 2**20),
        name="main",
    )(features, cotangent, ahead, back, short_filter, lines)


def factors_of(size):
    found = []
    factor = 2
    while size > 1:
        while size % factor == 0:
            found.append(factor)
            size //= factor
        factor += 1
    return found


def peers(value, axis, stride, factor):
    size = lax.axis_size(axis)
    got = []
    for turn in range(1, factor):
        route = []
        for i in range(size):
            digit = i // stride % factor
            route.append((i, i + ((digit + turn) % factor - digit) * stride))
        got.append(lax.ppermute(value, axis, route))
    return got


def add_in_order(value, got, axis, stride, factor):
    if factor == 2:
        return value.astype(F32) + got[0].astype(F32)
    digit = lax.axis_index(axis) // stride % factor
    every = jnp.stack([value] + got[::-1]).astype(F32)
    return jnp.sum(jnp.roll(every, digit, 0), 0)


def total_over(value, axis, stride, factors, kind):
    for factor in factors:
        value = value.astype(kind)
        value = add_in_order(value, peers(value, axis, stride, factor), axis, stride, factor)
        stride *= factor
    return value


def on_device(features, short_filter, long_filter, cotangent):
    _, rows, width = features.shape
    taps = short_filter.shape[1]
    groups, span = long_filter.shape
    members = width // groups
    per = LANES // members
    size = lax.axis_size("ctx")
    ahead, back = edges(features, cotangent, short_filter, span)
    ahead = lax.ppermute(ahead, "ctx", [(i, i + 1) for i in range(size - 1)])
    back = lax.ppermute(back, "ctx", [(i + 1, i) for i in range(size - 1)])
    rounded = long_filter.astype(BF16).astype(F32)
    lines = jnp.stack(
        [
            jnp.pad(rounded[:, ::-1], ((0, 0), (1, span - 1))),
            jnp.pad(rounded, ((0, 0), (0, span))),
        ]
    )
    grads, sums = main(features, cotangent, ahead, back, short_filter, lines, span, members)
    sums = total_over(sums, "ctx", 1, factors_of(size), BF16)
    square = jnp.sum(sums * sums)
    square = jnp.full((EDGE, LANES), square)
    square = total_over(square, "ch", 1, factors_of(lax.axis_size("ch")), F32)[:1, :1]
    factor = lax.rsqrt(square / (3 * taps * D + span * G) + 1e-06)
    scaled = sums * factor
    grad_short = scaled[: 3 * EDGE].reshape(3, EDGE, width)[:, :taps]
    grad_long = scaled[3 * EDGE :].reshape(per, width // LANES, span)
    return (grads, grad_short, grad_long.transpose(1, 0, 2).reshape(groups, span))


def solution(mesh):
    in_specs = (P(None, "ctx", "ch"), P(None, None, "ch"), P("ch", None), P("ctx", "ch"))
    out_specs = (P(None, "ctx", "ch"), P(None, None, "ch"), P("ch", None))
    return jax.shard_map(
        on_device, mesh=mesh, in_specs=in_specs, out_specs=out_specs, check_vma=False
    )
```

```python
import functools

import jax
import jax.numpy as jnp
from jax import lax
from jax.experimental import pallas as pl
from jax.experimental.pallas import tpu as pltpu
from jax.sharding import PartitionSpec as P

D = 8192
G = 512
LANES = 128
EDGE = 8
F32 = jnp.float32
BF16 = jnp.bfloat16


def taps_of(filt, which, lanes):
    return [filt[which, pl.ds(j, 1), lanes] for j in range(filt.shape[1])]


def conv(source, taps, base, count):
    total = None
    for j, tap in enumerate(taps):
        term = tap * source[pl.ds(base - j, count), :]
        total = term if total is None else total + term
    return total


def chunks(count, size):
    return [(at, min(size, count - at)) for at in range(0, count, size)]


def odd_place():
    return lax.rem(lax.axis_index("ctx"), 2)


def edge_kernel(span, feat, cot, filt, near, far, qx, kx, vx):
    rows = feat.shape[1]
    width = feat.shape[2]
    reach = span + 2 * EDGE

    def run(ahead, back):
        def tile(i, carry):
            lanes = pl.ds(pl.multiple_of(i * LANES, LANES), LANES)
            qx[...] = feat[0, 0:reach, lanes].astype(F32)
            kx[...] = feat[1, rows - reach : rows, lanes].astype(F32)
            vx[...] = feat[2, rows - reach : rows, lanes].astype(F32)
            fq, fk, fv = (taps_of(filt, a, lanes) for a in range(3))
            for at, size in chunks(span, 32):
                z = conv(kx, fk, at + 2 * EDGE, size) * conv(vx, fv, at + 2 * EDGE, size)
                ahead[at : at + size, lanes] = z.astype(BF16)
            q_tail = feat[0, rows - 2 * EDGE : rows, lanes].astype(F32)[EDGE:]
            k_tail = kx[reach - EDGE : reach, :]
            v_tail = vx[reach - EDGE : reach, :]
            tails = jnp.concatenate([q_tail, k_tail, v_tail, v_tail], 0)
            ahead[span : span + 4 * EDGE, lanes] = tails.astype(BF16)
            for at, size in chunks(span + EDGE, 32):
                low = max(at, EDGE)
                c = cot[at : at + max(size, 2 * EDGE), lanes].astype(F32)[low - at : size]
                dy = conv(qx, fq, low, at + size - low) * c
                if at == 0:
                    dy = jnp.concatenate([qx[0:EDGE, :], dy], 0)
                back[at : at + size, lanes] = dy.astype(BF16)
            heads = [feat[a, 0 : 2 * EDGE, lanes].astype(F32)[:EDGE] for a in (1, 2)]
            heads.append(cot[0 : 2 * EDGE, lanes].astype(F32)[:EDGE])
            back[span + EDGE : span + 4 * EDGE, lanes] = jnp.concatenate(heads, 0).astype(BF16)
            return carry

        lax.fori_loop(0, width // LANES, tile, 0)

    odd = odd_place()

    @pl.when(odd == 0)
    def _():
        run(near, far)

    @pl.when(odd == 1)
    def _():
        run(far, near)


def edges(features, cotangent, short_filter, span):
    _, rows, width = features.shape
    taps = short_filter.shape[1]
    step = min(width, 1024)
    return pl.pallas_call(
        functools.partial(edge_kernel, span),
        grid=(width // step,),
        in_specs=[
            pl.BlockSpec((3, rows, step), lambda i: (0, 0, i)),
            pl.BlockSpec((rows, step), lambda i: (0, i)),
            pl.BlockSpec((3, taps, step), lambda i: (0, 0, i)),
        ],
        out_specs=[pl.BlockSpec((span + 4 * EDGE, step), lambda i: (0, i))] * 2,
        out_shape=[jax.ShapeDtypeStruct((span + 4 * EDGE, width), BF16)] * 2,
        scratch_shapes=[pltpu.VMEM((span + 2 * EDGE, LANES), F32)] * 3,
        name="edges",
    )(features, cotangent, short_filter)


def band_kernel(span, lines, bands):
    for which in range(2):
        for g in range(lines.shape[1]):
            spread = jnp.broadcast_to(lines[which, g : g + 1, :], (span, 2 * span))
            turned = pltpu.roll(spread, 0, 1, stride=1, stride_axis=0)
            bands[which, g * span : (g + 1) * span, :] = turned.astype(BF16)


def toeplitz(lines, span):
    groups = lines.shape[1]
    step = min(groups, 16)
    return pl.pallas_call(
        functools.partial(band_kernel, span),
        grid=(groups // step,),
        in_specs=[pl.BlockSpec((2, step, 2 * span), lambda i: (0, i, 0))],
        out_specs=pl.BlockSpec((2, step * span, 2 * span), lambda i: (0, i, 0)),
        out_shape=jax.ShapeDtypeStruct((2, groups * span, 2 * span), BF16),
        cost_estimate=pl.CostEstimate(
            flops=0, bytes_accessed=8 * groups * span * span, transcendentals=0
        ),
        name="bands",
    )(lines)


def dot(a, b, dims=((1,), (0,))):
    return lax.dot_general(a, b, (dims, ((), ())), preferred_element_type=F32)


def main_kernel(
    span, members,
    feat, cot, near, far, filt, bands,
    grads, keep, send,
    qx, kx, vx, ksx, vsx, zx, dyx, dqx, dkx, dvx, zm, sums,
):
    rows = feat.shape[1]
    width = feat.shape[2]
    blocks = rows // span
    wide = rows + EDGE
    per = LANES // members
    small = span // 2
    pieces = rows // small
    odd = odd_place()

    @pl.when(pl.program_id(0) == 0)
    def _():
        zx[...] = jnp.zeros_like(zx)
        dyx[...] = jnp.zeros_like(dyx)

    def tile(i, carry):
        lanes = pl.ds(pl.multiple_of(i * LANES, LANES), LANES)
        fq, fk, fv = (taps_of(filt, a, lanes) for a in range(3))

        def ahead(low, high):
            return jnp.where(odd == 1, near[low:high, lanes], far[low:high, lanes])

        def back(low, high):
            return jnp.where(odd == 1, far[low:high, lanes], near[low:high, lanes])

        ends = ahead(span, span + 4 * EDGE).astype(F32)
        first = back(0, 2 * EDGE).astype(F32)
        last = back(span + EDGE, span + 4 * EDGE).astype(F32)
        for a, x in enumerate((qx, kx, vx)):
            x[0:EDGE, :] = ends[a * EDGE : (a + 1) * EDGE]
            for at, size in chunks(rows, 32):
                x[EDGE + at : EDGE + at + size, :] = feat[a, at : at + size, lanes].astype(F32)
        qx[EDGE + rows : EDGE + wide, :] = first[:EDGE]
        kx[EDGE + rows : EDGE + wide, :] = last[:EDGE]
        vx[EDGE + rows : EDGE + wide, :] = last[EDGE : 2 * EDGE]
        c_next = last[2 * EDGE :]

        for at, size in chunks(rows, 32):
            c = cot[at : at + size, lanes].astype(F32)
            dyx[at : at + size, :] = (c * conv(qx, fq, EDGE + at, size)).astype(BF16)
        dy_next = c_next * conv(qx, fq, EDGE + rows, EDGE)
        dyx[rows : rows + 2 * EDGE, :] = jnp.concatenate([dy_next, first[EDGE:]], 0).astype(BF16)
        dyx[rows + 2 * EDGE : rows + span + EDGE, :] = back(2 * EDGE, span + EDGE)
        zx[0:span, :] = ahead(0, span)
        for at, size in chunks(wide, 32):
            ks = conv(kx, fk, EDGE + at, size)
            vs = conv(vx, fv, EDGE + at, size)
            ksx[at : at + size, :] = ks
            vsx[at : at + size, :] = vs
            zx[span + at : span + at + size, :] = (ks * vs).astype(BF16)

        lane_group = lax.broadcasted_iota(jnp.int32, (1, LANES), 1) // members
        wide_group = jnp.concatenate([lane_group] * blocks, 1)

        def pick(stacked, size, owner):
            total = stacked[0:size]
            for g in range(1, per):
                total = jnp.where(owner == g, stacked[g * size : (g + 1) * size], total)
            return total

        def band(which):
            return bands[which, pl.ds(pl.multiple_of(i * per * span, span), per * span), :]

        def heads_of(which):
            return jnp.concatenate(
                [
                    bands[which, pl.ds(pl.multiple_of((i * per + g) * span, span), 2 * EDGE), :]
                    for g in range(per)
                ],
                0,
            )

        d_win = jnp.concatenate([dyx[b * span : (b + 2) * span, :] for b in range(blocks)], 1)
        dz = pick(dot(band(1), d_win), span, wide_group)
        dz_next = pick(dot(heads_of(1), dyx[rows : rows + 2 * span, :]), 2 * EDGE, lane_group)
        z_win = jnp.concatenate([zx[b * span : (b + 2) * span, :] for b in range(blocks)], 1)
        y = pick(dot(band(0), z_win), span, wide_group)
        y_next = pick(dot(heads_of(0), zx[rows : rows + 2 * span, :]), 2 * EDGE, lane_group)

        r = lax.broadcasted_iota(jnp.int32, (small, small), 0)
        s = lax.broadcasted_iota(jnp.int32, (small, small), 1)
        flip = jnp.where(r + s == small - 1, 1.0, 0.0).astype(BF16)
        z_own = jnp.concatenate(
            [zx[span + b * small : span + (b + 1) * small, :] for b in range(pieces)], 1
        )
        z_back = dot(flip, z_own).astype(BF16)
        piece_group = jnp.concatenate([lane_group] * pieces, 1)
        for g in range(per):
            kept = jnp.where(piece_group == g, z_back, jnp.zeros_like(z_back))
            zm[g * small : (g + 1) * small, :] = kept
        d_near = jnp.concatenate(
            [dyx[b * small : b * small + 2 * span, :] for b in range(pieces)], 1
        )
        pairs = dot(zm[...], d_near, ((1,), (1,)))

        def long_sum(g):
            part = pltpu.roll(
                pairs[g * small : (g + 1) * small, :],
                2 * span + 1 - small, 1, stride=1, stride_axis=0,
            )
            sums[1, EDGE + g : EDGE + g + 1, lanes] = jnp.sum(part[:, :span], 0, keepdims=True)

        for b in range(blocks):
            for at, size in chunks(span, 32):
                t = b * span + at
                piece = dz[at : at + size, b * LANES : (b + 1) * LANES]
                dkx[t : t + size, :] = piece * vsx[t : t + size, :]
                dvx[t : t + size, :] = piece * ksx[t : t + size, :]
        dkx[rows:wide, :] = dz_next[:EDGE] * vsx[rows:wide, :]
        dvx[rows:wide, :] = dz_next[:EDGE] * ksx[rows:wide, :]
        for b in range(blocks):
            for at, size in chunks(span, 32):
                t = b * span + at
                c = cot[t : t + size, lanes].astype(F32)
                dqx[t : t + size, :] = c * y[at : at + size, b * LANES : (b + 1) * LANES]
        dqx[rows:wide, :] = c_next * y_next[:EDGE]

        done = 0
        for a, (x, dx, taps) in enumerate(((qx, dqx, fq), (kx, dkx, fk), (vx, dvx, fv))):
            parts = [None] * len(taps)
            for at, size in chunks(rows, 32):
                own = x[EDGE + at : EDGE + at + size, :]
                total = None
                for j, tap in enumerate(taps):
                    moved = dx[pl.ds(at + j, size), :]
                    term = tap * moved
                    total = term if total is None else total + term
                    prod = jnp.sum((own * moved).reshape(size // EDGE, EDGE, LANES), 0)
                    parts[j] = prod if parts[j] is None else parts[j] + prod
                grads[a, at : at + size, lanes] = total.astype(BF16)
                if done < per:
                    long_sum(done)
                    done += 1
            found = [jnp.sum(p, 0, keepdims=True) for p in parts]
            found.append(jnp.zeros((EDGE - len(taps), LANES), F32))
            sums[a // 2, a % 2 * EDGE : (a % 2 + 1) * EDGE, lanes] = jnp.concatenate(found, 0)
        for g in range(done, per):
            long_sum(g)
        return carry

    lax.fori_loop(0, width // LANES, tile, 0)
    keep[...] = sums[odd].astype(BF16)
    send[...] = sums[1 - odd].astype(BF16)


def main(features, cotangent, near, far, short_filter, bands, span, members):
    _, rows, width = features.shape
    taps = short_filter.shape[1]
    step = min(width, 512)
    per = LANES // members
    wide = rows + EDGE
    tall = rows + 2 * span
    half = (3 * EDGE + per) // 2
    return pl.pallas_call(
        functools.partial(main_kernel, span, members),
        grid=(width // step,),
        in_specs=[
            pl.BlockSpec((3, rows, step), lambda i: (0, 0, i)),
            pl.BlockSpec((rows, step), lambda i: (0, i)),
            pl.BlockSpec((span + 4 * EDGE, step), lambda i: (0, i)),
            pl.BlockSpec((span + 4 * EDGE, step), lambda i: (0, i)),
            pl.BlockSpec((3, taps, step), lambda i: (0, 0, i)),
            pl.BlockSpec((2, step // members * span, 2 * span), lambda i: (0, i, 0)),
        ],
        out_specs=[
            pl.BlockSpec((3, rows, step), lambda i: (0, 0, i)),
            pl.BlockSpec((half, step), lambda i: (0, i)),
            pl.BlockSpec((half, step), lambda i: (0, i)),
        ],
        out_shape=[
            jax.ShapeDtypeStruct((3, rows, width), BF16),
            jax.ShapeDtypeStruct((half, width), BF16),
            jax.ShapeDtypeStruct((half, width), BF16),
        ],
        scratch_shapes=[pltpu.VMEM((wide + EDGE, LANES), F32)] * 3
        + [pltpu.VMEM((wide, LANES), F32)] * 2
        + [pltpu.VMEM((tall, LANES), BF16)] * 2
        + [pltpu.VMEM((wide, LANES), F32)] * 3
        + [pltpu.VMEM((per * span // 2, 2 * rows // span * LANES), BF16)]
        + [pltpu.VMEM((2, half, step), F32)],
        compiler_params=pltpu.CompilerParams(vmem_limit_bytes=67043328),
        name="main",
    )(features, cotangent, near, far, short_filter, bands)


def finish_kernel(count, span, own, other, squares, grad_short, grad_long):
    odd = odd_place()
    taps = grad_short.shape[1]
    width = own.shape[1]
    per = own.shape[0] - EDGE
    total = jnp.sum(jnp.sum(squares[...], 0, keepdims=True), 1, keepdims=True)
    factor = lax.rsqrt(total / count + 1e-06)

    def put(low, high):
        grad_short[0] = low[0:taps, :] * factor
        grad_short[1] = low[EDGE : EDGE + taps, :] * factor
        grad_short[2] = high[0:taps, :] * factor
        for i in range(width // LANES):
            grad_long[i * per : (i + 1) * per, :] = (
                high[EDGE : EDGE + per, i * LANES : (i + 1) * LANES] * factor
            )

    @pl.when(odd == 0)
    def _():
        put(own, other)

    @pl.when(odd == 1)
    def _():
        put(other, own)


def finish(own, other, squares, taps, groups, span, count):
    width = own.shape[1]
    return pl.pallas_call(
        functools.partial(finish_kernel, count, span),
        out_shape=[
            jax.ShapeDtypeStruct((3, taps, width), F32),
            jax.ShapeDtypeStruct((groups, span), F32),
        ],
        name="finish",
    )(own, other, squares)


def square_kernel(own, other, out):
    total = None
    for x in (own, other):
        for at in range(0, x.shape[1], LANES):
            piece = x[:, at : at + LANES]
            square = jnp.sum((piece * piece).reshape(-1, EDGE, LANES), 0)
            total = square if total is None else total + square
    out[...] = total


def squares_of(own, other):
    return pl.pallas_call(
        square_kernel, out_shape=jax.ShapeDtypeStruct((EDGE, LANES), F32), name="squares"
    )(own, other)


def factors_of(size):
    found = []
    factor = 4
    while size > 1:
        while size % factor == 0:
            found.append(factor)
            size //= factor
        factor = 2 if factor == 4 else factor + 1
    return found


def swap(value, axis, stride, factor, turn):
    route = []
    for i in range(lax.axis_size(axis)):
        digit = i // stride % factor
        other = digit ^ turn if factor in (2, 4) else (digit + turn) % factor
        route.append((i, i + (other - digit) * stride))
    return lax.ppermute(value, axis, route)


def total_over(value, axis, stride, size, kind):
    value = value.astype(F32)
    for factor in factors_of(size):
        sent = value.astype(kind)
        got = [sent] + [swap(sent, axis, stride, factor, turn) for turn in range(1, factor)]
        got = [part.astype(F32) for part in got]
        if factor == 2:
            value = got[0] + got[1]
        elif factor == 4:
            value = (got[0] + got[1]) + (got[2] + got[3])
        else:
            digit = lax.axis_index(axis) // stride % factor
            every = jnp.stack(got[:1] + got[:0:-1])
            ordered = jnp.roll(every, -((factor - digit) % factor), 0)
            value = ordered[0]
            for part in ordered[1:]:
                value = value + part
        stride *= factor
    return value


def on_device(features, short_filter, long_filter, cotangent):
    _, rows, width = features.shape
    taps = short_filter.shape[1]
    groups, span = long_filter.shape
    members = width // groups
    size = lax.axis_size("ctx")
    near, far = edges(features, cotangent, short_filter, span)
    near = lax.ppermute(near, "ctx", [(i, i ^ 1) for i in range(size)])
    far = lax.ppermute(far, "ctx", [(i, (i + 1 ^ 1) - 1) for i in range(1, size - 1)])
    rounded = long_filter.astype(BF16).astype(F32)
    lines = jnp.stack(
        [
            jnp.pad(rounded[:, ::-1], ((0, 0), (1, span - 1))),
            jnp.pad(rounded, ((0, 0), (0, span))),
        ]
    )
    bands = toeplitz(lines, span)
    grads, keep, send = main(
        features, cotangent, near, far, short_filter, bands, span, members
    )
    own = keep.astype(F32) + swap(send, "ctx", 1, 2, 1).astype(F32)
    own = total_over(own, "ctx", 2, size // 2, BF16)
    other = swap(own, "ctx", 1, 2, 1)
    squares = total_over(squares_of(own, other), "ch", 1, lax.axis_size("ch"), F32)
    count = 3 * taps * D + span * G
    grad_short, grad_long = finish(own, other, squares, taps, groups, span, count)
    return (grads, grad_short, grad_long)


def solution(mesh):
    in_specs = (P(None, "ctx", "ch"), P(None, None, "ch"), P("ch", None), P("ctx", "ch"))
    out_specs = (P(None, "ctx", "ch"), P(None, None, "ch"), P("ch", None))
    return jax.shard_map(
        on_device, mesh=mesh, in_specs=in_specs, out_specs=out_specs, check_vma=False
    )
```

```python
import functools

import jax
import jax.numpy as jnp
from jax import lax
from jax.experimental import pallas as pl
from jax.experimental.pallas import tpu as pltpu
from jax.sharding import PartitionSpec as P

D = 8192
G = 512
LANES = 128
EDGE = 8
F32 = jnp.float32
BF16 = jnp.bfloat16


def taps_of(filt, which, lanes):
    return [filt[which, pl.ds(j, 1), lanes] for j in range(filt.shape[1])]


def conv(source, taps, base, count):
    total = None
    for j, tap in enumerate(taps):
        term = tap * source[pl.ds(base - j, count), :]
        total = term if total is None else total + term
    return total


def chunks(count, size):
    return [(at, min(size, count - at)) for at in range(0, count, size)]


def odd_place():
    return lax.rem(lax.axis_index("ctx"), 2)


def edge_kernel(span, feat, cot, filt, near, far, qx, kx, vx):
    rows = feat.shape[1]
    width = feat.shape[2]
    reach = span + 2 * EDGE

    def run(ahead, back):
        def tile(i, carry):
            lanes = pl.ds(pl.multiple_of(i * LANES, LANES), LANES)
            qx[...] = feat[0, 0:reach, lanes].astype(F32)
            kx[...] = feat[1, rows - reach : rows, lanes].astype(F32)
            vx[...] = feat[2, rows - reach : rows, lanes].astype(F32)
            fq, fk, fv = (taps_of(filt, a, lanes) for a in range(3))
            for at, size in chunks(span, 32):
                z = conv(kx, fk, at + 2 * EDGE, size) * conv(vx, fv, at + 2 * EDGE, size)
                ahead[at : at + size, lanes] = z.astype(BF16)
            q_tail = feat[0, rows - 2 * EDGE : rows, lanes].astype(F32)[EDGE:]
            k_tail = kx[reach - EDGE : reach, :]
            v_tail = vx[reach - EDGE : reach, :]
            tails = jnp.concatenate([q_tail, k_tail, v_tail, v_tail], 0)
            ahead[span : span + 4 * EDGE, lanes] = tails.astype(BF16)
            for at, size in chunks(span + EDGE, 32):
                low = max(at, EDGE)
                c = cot[at : at + max(size, 2 * EDGE), lanes].astype(F32)[low - at : size]
                dy = conv(qx, fq, low, at + size - low) * c
                if at == 0:
                    dy = jnp.concatenate([qx[0:EDGE, :], dy], 0)
                back[at : at + size, lanes] = dy.astype(BF16)
            heads = [feat[a, 0 : 2 * EDGE, lanes].astype(F32)[:EDGE] for a in (1, 2)]
            heads.append(cot[0 : 2 * EDGE, lanes].astype(F32)[:EDGE])
            back[span + EDGE : span + 4 * EDGE, lanes] = jnp.concatenate(heads, 0).astype(BF16)
            return carry

        lax.fori_loop(0, width // LANES, tile, 0)

    odd = odd_place()

    @pl.when(odd == 0)
    def _():
        run(near, far)

    @pl.when(odd == 1)
    def _():
        run(far, near)


def edges(features, cotangent, short_filter, span):
    _, rows, width = features.shape
    taps = short_filter.shape[1]
    step = min(width, 1024)
    return pl.pallas_call(
        functools.partial(edge_kernel, span),
        grid=(width // step,),
        in_specs=[
            pl.BlockSpec((3, rows, step), lambda i: (0, 0, i)),
            pl.BlockSpec((rows, step), lambda i: (0, i)),
            pl.BlockSpec((3, taps, step), lambda i: (0, 0, i)),
        ],
        out_specs=[pl.BlockSpec((span + 4 * EDGE, step), lambda i: (0, i))] * 2,
        out_shape=[jax.ShapeDtypeStruct((span + 4 * EDGE, width), BF16)] * 2,
        scratch_shapes=[pltpu.VMEM((span + 2 * EDGE, LANES), F32)] * 3,
        name="edges",
    )(features, cotangent, short_filter)


def dot(a, b, dims=((1,), (0,))):
    return lax.dot_general(a, b, (dims, ((), ())), preferred_element_type=F32)


def owners(members, count):
    lane = lax.broadcasted_iota(jnp.int32, (1, LANES), 1) // members
    return jnp.concatenate([lane] * count, 1) if count > 1 else lane


def pick(stacked, size, owner, per):
    total = stacked[0:size]
    for g in range(1, per):
        total = jnp.where(owner == g, stacked[g * size : (g + 1) * size], total)
    return total


def strip(filters, g, shift):
    row = filters[g : g + 1, :]
    spread = jnp.concatenate([row, jnp.zeros_like(row)], 1)
    spread = jnp.broadcast_to(spread, (2 * EDGE, spread.shape[1]))
    return pltpu.roll(spread, shift, 1, stride=1, stride_axis=0).astype(BF16)


def reversing(size):
    r = lax.broadcasted_iota(jnp.int32, (size, size), 0)
    s = lax.broadcasted_iota(jnp.int32, (size, size), 1)
    return jnp.where(r + s == size - 1, 1.0, 0.0).astype(BF16)


def fill_band(out, g, base, span, per):
    rows = 2 * EDGE
    for at in range(0, span, rows):
        moved = base if at == 0 else pltpu.roll(base, at, 1)
        start = at * per + g * rows
        out[start : start + rows, :] = moved


def flipped(pieces, small):
    return dot(reversing(small), jnp.concatenate(pieces, 1)).astype(BF16)


def diagonal_sum(pairs, g, small, span):
    part = pltpu.roll(
        pairs[g * small : (g + 1) * small, :], 2 * span + 1 - small, 1, stride=1, stride_axis=0
    )
    return jnp.sum(part[:, :span], 0, keepdims=True)


def woven(first, second):
    live = [first, second]
    while live:
        for job in list(live):
            if next(job, True):
                live.remove(job)


def own_kernel(span, feat, cot, filt, ks_out, vs_out, z_out, dy_out, qx, kx, vx):
    rows = feat.shape[1]
    width = feat.shape[2]

    def tile(i, carry):
        lanes = pl.ds(pl.multiple_of(i * LANES, LANES), LANES)
        fq, fk, fv = (taps_of(filt, a, lanes) for a in range(3))
        for a, x in enumerate((qx, kx, vx)):
            for at, size in chunks(rows, 32):
                x[at : at + size, :] = feat[a, at : at + size, lanes].astype(F32)
        hole = jnp.zeros((EDGE, LANES), F32)
        for at, size in chunks(rows, 32):
            low = max(at, EDGE)
            c = cot[at : at + size, lanes].astype(F32)[low - at :]
            dy = c * conv(qx, fq, low, at + size - low)
            ks = conv(kx, fk, low, at + size - low)
            vs = conv(vx, fv, low, at + size - low)
            z = ks * vs
            ks_out[low : at + size, lanes] = ks
            vs_out[low : at + size, lanes] = vs
            if at == 0:
                z, dy = (jnp.concatenate([hole, x], 0) for x in (z, dy))
            z_out[at : at + size, lanes] = z.astype(BF16)
            dy_out[at : at + size, lanes] = dy.astype(BF16)
        return carry

    @pl.when(pl.program_id(0) >= 0)
    def _():
        ks_out[0:EDGE, :] = jnp.zeros((EDGE, width), F32)
        vs_out[0:EDGE, :] = jnp.zeros((EDGE, width), F32)

    lax.fori_loop(0, width // LANES, tile, 0)


def column_spec(step, *shape):
    return pl.BlockSpec(shape + (step,), lambda i: (0,) * len(shape) + (i,))


def own_part(features, cotangent, short_filter, span):
    _, rows, width = features.shape
    taps = short_filter.shape[1]
    step = min(width, 512)
    column = functools.partial(column_spec, step)
    kinds = [F32, F32, BF16, BF16]
    return pl.pallas_call(
        functools.partial(own_kernel, span),
        grid=(width // step,),
        in_specs=[column(3, rows), column(rows), column(3, taps)],
        out_specs=[column(rows)] * 4,
        out_shape=[jax.ShapeDtypeStruct((rows, width), kind) for kind in kinds],
        scratch_shapes=[pltpu.VMEM((rows, LANES), F32)] * 3,
        compiler_params=pltpu.CompilerParams(vmem_limit_bytes=67043328),
        cost_estimate=pl.CostEstimate(
            flops=40 * rows * width, bytes_accessed=20 * rows * width, transcendentals=0
        ),
        name="own",
    )(features, cotangent, short_filter)


def join_kernel(
    span, members,
    feat, cot, near, far, filt, lines, ks_in, vs_in, z_in, dy_in,
    grads, keep, send, sums, *scratch,
):
    rows = feat.shape[1]
    width = feat.shape[2]
    per = LANES // members
    blocks = rows // span
    small = span // 2
    wide = rows + EDGE
    odd = odd_place()
    count = len(scratch) // 2
    sets = (scratch[:count], scratch[count:])

    @pl.when(pl.program_id(0) == 0)
    def _():
        for bufs in sets:
            for ref in bufs[3:5]:
                ref[...] = jnp.zeros_like(ref)

    hole = jnp.zeros((EDGE, LANES), F32)

    def halves(low, high):
        return jnp.concatenate([low, high], 0).astype(BF16)

    def column(i):
        return pl.ds(i * LANES, LANES)

    def first_stage(i, bufs):
        qx, kx, vx, zx, dyx, dqx, dkx, dvx, tst, ust, zm, pairs = bufs
        lanes = column(i)
        fq, fk, fv = (taps_of(filt, a, lanes) for a in range(3))

        def ahead(low, high):
            return jnp.where(odd == 1, near[low:high, lanes], far[low:high, lanes])

        def back(low, high):
            return jnp.where(odd == 1, far[low:high, lanes], near[low:high, lanes])

        ends = ahead(span, span + 4 * EDGE).astype(F32)
        first = back(0, 2 * EDGE).astype(F32)
        last = back(span + EDGE, span + 4 * EDGE).astype(F32)
        nexts = (first[:EDGE], last[:EDGE], last[EDGE : 2 * EDGE])
        c_next = last[2 * EDGE :]
        c_first = cot[0 : 2 * EDGE, lanes].astype(F32)[:EDGE]
        for a, x in enumerate((qx, kx, vx)):
            x[0:EDGE, :] = ends[a * EDGE : (a + 1) * EDGE]
            x[EDGE : 2 * EDGE, :] = feat[a, 0 : 2 * EDGE, lanes].astype(F32)[:EDGE]
            x[2 * EDGE : 3 * EDGE, :] = feat[a, rows - 2 * EDGE : rows, lanes].astype(F32)[EDGE:]
            x[3 * EDGE : 4 * EDGE, :] = nexts[a]
        dy_first = c_first * conv(qx, fq, EDGE, EDGE)
        dy_next = c_next * conv(qx, fq, 3 * EDGE, EDGE)
        ks_first, vs_first = conv(kx, fk, EDGE, EDGE), conv(vx, fv, EDGE, EDGE)
        ks_next, vs_next = conv(kx, fk, 3 * EDGE, EDGE), conv(vx, fv, 3 * EDGE, EDGE)
        top = slice(0, 2 * EDGE)
        dyx[0 : 2 * EDGE, :] = halves(dy_first, dy_in[top, lanes].astype(F32)[EDGE:])
        dyx[2 * EDGE : rows, :] = dy_in[2 * EDGE : rows, lanes]
        dyx[rows : rows + 2 * EDGE, :] = halves(dy_next, first[EDGE:])
        dyx[rows + 2 * EDGE : rows + span + EDGE, :] = back(2 * EDGE, span + EDGE)
        zx[0:span, :] = ahead(0, span)
        z_top = halves(ks_first * vs_first, z_in[top, lanes].astype(F32)[EDGE:])
        zx[span : span + 2 * EDGE, :] = z_top
        zx[span + 2 * EDGE : span + rows, :] = z_in[2 * EDGE : rows, lanes]
        zx[span + rows : span + rows + 2 * EDGE, :] = halves(ks_next * vs_next, hole)

        owner = owners(members, blocks)
        one = owners(members, 1)
        rows16 = 2 * EDGE

        def windows(ref):
            return jnp.concatenate([ref[b * span : (b + 2) * span, :] for b in range(blocks)], 1)

        def chunk_of(stacked, at, who):
            start = at * per
            return pick(stacked[start : start + rows16 * per], rows16, who, per)

        filters = lines[i * per : (i + 1) * per, :].astype(BF16)
        turned = dot(filters, reversing(span))
        filters = filters.astype(F32)
        for g in range(per):
            fill_band(ust, g, strip(filters, g, 0), span, per)
            yield False
        dz = dot(ust[...], windows(dyx))
        dz_next = chunk_of(dot(ust[0 : rows16 * per, :], dyx[rows : rows + 2 * span, :]), 0, one)
        dkx[rows:wide, :] = dz_next[:EDGE] * vs_next
        dvx[rows:wide, :] = dz_next[:EDGE] * ks_next
        left = list(range(per))
        for at in range(0, span, rows16):
            piece = chunk_of(dz, at, owner)
            for b in range(blocks):
                t = b * span + at
                part = piece[:, b * LANES : (b + 1) * LANES]
                vs, ks = vs_in[t : t + rows16, lanes], ks_in[t : t + rows16, lanes]
                if t == 0:
                    vs = jnp.concatenate([vs_first, vs[EDGE:]], 0)
                    ks = jnp.concatenate([ks_first, ks[EDGE:]], 0)
                dkx[t : t + rows16, :] = part * vs
                dvx[t : t + rows16, :] = part * ks
            if left:
                g = left.pop(0)
                fill_band(tst, g, strip(turned, g, 1), span, per)
            yield False
        for g in left:
            fill_band(tst, g, strip(turned, g, 1), span, per)
        y = dot(tst[...], windows(zx))
        y_next = chunk_of(dot(tst[0 : rows16 * per, :], zx[rows : rows + 2 * span, :]), 0, one)
        dqx[rows:wide, :] = c_next * y_next[:EDGE]
        starts = range(0, rows, small)
        z_back = flipped([zx[span + t : span + t + small, :] for t in starts], small)
        who = owners(members, len(starts))
        left = list(range(per))

        def mask(g):
            kept = jnp.where(who == g, 1.0, 0.0).astype(BF16)
            zm[g * small : (g + 1) * small, :] = z_back * kept

        for at in range(0, span, rows16):
            piece = chunk_of(y, at, owner)
            for b in range(blocks):
                t = b * span + at
                c = cot[t : t + rows16, lanes].astype(F32)
                dqx[t : t + rows16, :] = c * piece[:, b * LANES : (b + 1) * LANES]
            if left:
                mask(left.pop(0))
            yield False
        for g in left:
            mask(g)
        near_rows = jnp.concatenate([dyx[t : t + 2 * span, :] for t in starts], 1)
        pairs[...] = dot(zm[...], near_rows, ((1,), (1,)))

    def second_stage(i, bufs):
        qx, kx, vx, zx, dyx, dqx, dkx, dvx, tst, ust, zm, pairs = bufs
        lanes = column(i)
        left = list(range(per))

        def diagonal(g):
            sums[1, EDGE + g : EDGE + g + 1, lanes] = diagonal_sum(pairs, g, small, span)

        for a, dx in zip((1, 2, 0), (dkx, dvx, dqx)):
            taps = taps_of(filt, a, lanes)
            parts = [None] * len(taps)
            for at, size in chunks(rows, 32):
                own = feat[a, at : at + size, lanes].astype(F32)
                total = None
                for j, tap in enumerate(taps):
                    moved = dx[pl.ds(at + j, size), :]
                    term = tap * moved
                    total = term if total is None else total + term
                    prod = jnp.sum((own * moved).reshape(size // EDGE, EDGE, LANES), 0)
                    parts[j] = prod if parts[j] is None else parts[j] + prod
                grads[a, at : at + size, lanes] = total.astype(BF16)
                if left:
                    diagonal(left.pop(0))
                yield False
            found = [jnp.sum(p, 0, keepdims=True) for p in parts]
            found.append(jnp.zeros((EDGE - len(taps), LANES), F32))
            sums[a // 2, a % 2 * EDGE : (a % 2 + 1) * EDGE, lanes] = jnp.concatenate(found, 0)
        for g in left:
            diagonal(g)

    tiles = width // LANES
    woven(first_stage(0, sets[0]), iter(()))

    for i in range(tiles):
        after = first_stage(i + 1, sets[(i + 1) % 2]) if i + 1 < tiles else iter(())
        woven(after, second_stage(i, sets[i % 2]))
    keep[...] = sums[odd].astype(BF16)
    send[...] = sums[1 - odd].astype(BF16)


def join(features, cotangent, got, short_filter, long_filter, parts, span, members):
    _, rows, width = features.shape
    taps = short_filter.shape[1]
    step = min(width, 1024)
    per = LANES // members
    wide = rows + EDGE
    tall = rows + 2 * span
    half = (3 * EDGE + per) // 2
    column = functools.partial(column_spec, step)
    buffers = (
        [pltpu.VMEM((4 * EDGE, LANES), F32)] * 3
        + [pltpu.VMEM((tall, LANES), BF16)] * 2
        + [pltpu.VMEM((wide, LANES), F32)] * 3
        + [pltpu.VMEM((per * span, 2 * span), BF16)] * 2
        + [pltpu.VMEM((per * span // 2, 2 * rows // span * LANES), BF16)]
        + [pltpu.VMEM((per * span // 2, 2 * span), F32)]
    )
    return pl.pallas_call(
        functools.partial(join_kernel, span, members),
        grid=(width // step,),
        in_specs=[
            column(3, rows),
            column(rows),
            column(span + 4 * EDGE),
            column(span + 4 * EDGE),
            column(3, taps),
            pl.BlockSpec((step // members, span), lambda i: (i, 0)),
            *[column(rows)] * 4,
        ],
        out_specs=[column(3, rows), column(half), column(half)],
        out_shape=[
            jax.ShapeDtypeStruct((3, rows, width), BF16),
            jax.ShapeDtypeStruct((half, width), BF16),
            jax.ShapeDtypeStruct((half, width), BF16),
        ],
        scratch_shapes=[pltpu.VMEM((2, half, step), F32)] + buffers * 2,
        compiler_params=pltpu.CompilerParams(vmem_limit_bytes=67043328),
        name="join",
    )(features, cotangent, *got, short_filter, long_filter, *parts)


def finish_kernel(count, own, other, *refs):
    *squares, grad_short, grad_long = refs
    odd = odd_place()
    taps = grad_short.shape[1]
    width = own.shape[1]
    per = own.shape[0] - EDGE
    found = [ref[...] for ref in squares]
    while len(found) > 1:
        found = [sum(found[at : at + 2]) for at in range(0, len(found), 2)]
    total = jnp.sum(jnp.sum(found[0], 0, keepdims=True), 1, keepdims=True)
    factor = lax.rsqrt(total / count + 1e-06)

    def put(low, high):
        grad_short[0] = low[0:taps, :] * factor
        grad_short[1] = low[EDGE : EDGE + taps, :] * factor
        grad_short[2] = high[0:taps, :] * factor
        for i in range(width // LANES):
            grad_long[i * per : (i + 1) * per, :] = (
                high[EDGE : EDGE + per, i * LANES : (i + 1) * LANES] * factor
            )

    @pl.when(odd == 0)
    def _():
        put(own, other)

    @pl.when(odd == 1)
    def _():
        put(other, own)


def finish(own, other, squares, taps, groups, span, count):
    width = own.shape[1]
    return pl.pallas_call(
        functools.partial(finish_kernel, count),
        out_shape=[
            jax.ShapeDtypeStruct((3, taps, width), F32),
            jax.ShapeDtypeStruct((groups, span), F32),
        ],
        name="finish",
    )(own, other, *squares)


def square_kernel(own, other, out):
    total = None
    for x in (own, other):
        for at in range(0, x.shape[1], LANES):
            piece = x[:, at : at + LANES]
            square = jnp.sum((piece * piece).reshape(-1, EDGE, LANES), 0)
            total = square if total is None else total + square
    out[...] = total


def squares_of(own, other):
    return pl.pallas_call(
        square_kernel, out_shape=jax.ShapeDtypeStruct((EDGE, LANES), F32), name="squares"
    )(own, other)


def factors_of(size):
    found = []
    factor = 4
    while size > 1:
        while size % factor == 0:
            found.append(factor)
            size //= factor
        factor = 2 if factor == 4 else factor + 1
    return found


def swap(value, axis, stride, factor, turn):
    route = []
    for i in range(lax.axis_size(axis)):
        digit = i // stride % factor
        other = digit ^ turn if factor in (2, 4) else (digit + turn) % factor
        route.append((i, i + (other - digit) * stride))
    return lax.ppermute(value, axis, route)


def total_over(value, axis, stride, size, kind):
    value = value.astype(F32)
    for factor in factors_of(size):
        sent = value.astype(kind)
        got = [sent] + [swap(sent, axis, stride, factor, turn) for turn in range(1, factor)]
        got = [part.astype(F32) for part in got]
        if factor == 2:
            value = got[0] + got[1]
        elif factor == 4:
            value = (got[0] + got[1]) + (got[2] + got[3])
        else:
            digit = lax.axis_index(axis) // stride % factor
            every = jnp.stack(got[:1] + got[:0:-1])
            ordered = jnp.roll(every, -((factor - digit) % factor), 0)
            value = ordered[0]
            for part in ordered[1:]:
                value = value + part
        stride *= factor
    return value


def on_device(features, short_filter, long_filter, cotangent):
    _, rows, width = features.shape
    taps = short_filter.shape[1]
    groups, span = long_filter.shape
    members = width // groups
    size = lax.axis_size("ctx")
    near, far = edges(features, cotangent, short_filter, span)
    got = (
        lax.ppermute(near, "ctx", [(i, i ^ 1) for i in range(size)]),
        lax.ppermute(far, "ctx", [(i, (i + 1 ^ 1) - 1) for i in range(1, size - 1)]),
    )
    parts = own_part(features, cotangent, short_filter, span)
    grads, keep, send = join(
        features, cotangent, got, short_filter, long_filter, parts, span, members
    )
    own = keep.astype(F32) + swap(send, "ctx", 1, 2, 1).astype(F32)
    own = total_over(own, "ctx", 2, size // 2, BF16)
    other = swap(own, "ctx", 1, 2, 1)
    *early, late = factors_of(lax.axis_size("ch"))
    squares = squares_of(own, other)
    stride = 1
    for factor in early:
        squares = total_over(squares, "ch", stride, factor, F32)
        stride *= factor
    squares = [squares] + [swap(squares, "ch", stride, late, turn) for turn in range(1, late)]
    count = 3 * taps * D + span * G
    grad_short, grad_long = finish(own, other, squares, taps, groups, span, count)
    return (grads, grad_short, grad_long)


def solution(mesh):
    in_specs = (P(None, "ctx", "ch"), P(None, None, "ch"), P("ch", None), P("ctx", "ch"))
    out_specs = (P(None, "ctx", "ch"), P(None, None, "ch"), P("ch", None))
    return jax.shard_map(
        on_device, mesh=mesh, in_specs=in_specs, out_specs=out_specs, check_vma=False
    )
```

```python
import functools

import jax
import jax.numpy as jnp
from jax import lax
from jax.experimental import pallas as pl
from jax.experimental.pallas import tpu as pltpu
from jax.sharding import PartitionSpec as P

D = 8192
G = 512
LANES = 128
EDGE = 8
F32 = jnp.float32
BF16 = jnp.bfloat16


def taps_of(filt, which, lanes):
    return [filt[which, pl.ds(j, 1), lanes] for j in range(filt.shape[1])]


def conv(source, taps, base, count):
    total = None
    for j, tap in enumerate(taps):
        term = tap * source[pl.ds(base - j, count), :]
        total = term if total is None else total + term
    return total


def chunks(count, size):
    return [(at, min(size, count - at)) for at in range(0, count, size)]


def odd_place():
    return lax.rem(lax.axis_index("ctx"), 2)


def edge_kernel(span, feat, cot, filt, near, far, qx, kx, vx):
    rows = feat.shape[1]
    width = feat.shape[2]
    reach = span + 2 * EDGE

    def run(ahead, back):
        def tile(i, carry):
            lanes = pl.ds(pl.multiple_of(i * LANES, LANES), LANES)
            qx[...] = feat[0, 0:reach, lanes].astype(F32)
            kx[...] = feat[1, rows - reach : rows, lanes].astype(F32)
            vx[...] = feat[2, rows - reach : rows, lanes].astype(F32)
            fq, fk, fv = (taps_of(filt, a, lanes) for a in range(3))
            for at, size in chunks(span, 32):
                z = conv(kx, fk, at + 2 * EDGE, size) * conv(vx, fv, at + 2 * EDGE, size)
                ahead[at : at + size, lanes] = z.astype(BF16)
            q_tail = feat[0, rows - 2 * EDGE : rows, lanes].astype(F32)[EDGE:]
            k_tail = kx[reach - EDGE : reach, :]
            v_tail = vx[reach - EDGE : reach, :]
            tails = jnp.concatenate([q_tail, k_tail, v_tail, v_tail], 0)
            ahead[span : span + 4 * EDGE, lanes] = tails.astype(BF16)
            for at, size in chunks(span + EDGE, 32):
                low = max(at, EDGE)
                c = cot[at : at + max(size, 2 * EDGE), lanes].astype(F32)[low - at : size]
                dy = conv(qx, fq, low, at + size - low) * c
                if at == 0:
                    dy = jnp.concatenate([qx[0:EDGE, :], dy], 0)
                back[at : at + size, lanes] = dy.astype(BF16)
            heads = [feat[a, 0 : 2 * EDGE, lanes].astype(F32)[:EDGE] for a in (1, 2)]
            heads.append(cot[0 : 2 * EDGE, lanes].astype(F32)[:EDGE])
            back[span + EDGE : span + 4 * EDGE, lanes] = jnp.concatenate(heads, 0).astype(BF16)
            return carry

        lax.fori_loop(0, width // LANES, tile, 0)

    odd = odd_place()

    @pl.when(odd == 0)
    def _():
        run(near, far)

    @pl.when(odd == 1)
    def _():
        run(far, near)


def edges(features, cotangent, short_filter, span):
    _, rows, width = features.shape
    taps = short_filter.shape[1]
    step = min(width, 1024)
    return pl.pallas_call(
        functools.partial(edge_kernel, span),
        grid=(width // step,),
        in_specs=[
            pl.BlockSpec((3, rows, step), lambda i: (0, 0, i)),
            pl.BlockSpec((rows, step), lambda i: (0, i)),
            pl.BlockSpec((3, taps, step), lambda i: (0, 0, i)),
        ],
        out_specs=[pl.BlockSpec((span + 4 * EDGE, step), lambda i: (0, i))] * 2,
        out_shape=[jax.ShapeDtypeStruct((span + 4 * EDGE, width), BF16)] * 2,
        scratch_shapes=[pltpu.VMEM((span + 2 * EDGE, LANES), F32)] * 3,
        name="edges",
    )(features, cotangent, short_filter)


def dot(a, b, dims=((1,), (0,))):
    return lax.dot_general(a, b, (dims, ((), ())), preferred_element_type=F32)


def owners(members, count):
    lane = lax.broadcasted_iota(jnp.int32, (1, LANES), 1) // members
    return jnp.concatenate([lane] * count, 1) if count > 1 else lane


def pick(stacked, size, owner, per):
    total = stacked[0:size]
    for g in range(1, per):
        total = jnp.where(owner == g, stacked[g * size : (g + 1) * size], total)
    return total


def strip(filters, g, shift):
    row = filters[g : g + 1, :]
    spread = jnp.concatenate([row, jnp.zeros_like(row)], 1)
    spread = jnp.broadcast_to(spread, (2 * EDGE, spread.shape[1]))
    return pltpu.roll(spread, shift, 1, stride=1, stride_axis=0).astype(BF16)


def reversing(size):
    r = lax.broadcasted_iota(jnp.int32, (size, size), 0)
    s = lax.broadcasted_iota(jnp.int32, (size, size), 1)
    return jnp.where(r + s == size - 1, 1.0, 0.0).astype(BF16)


def fill_band(out, g, base, span, per):
    rows = 2 * EDGE
    for at in range(0, span, rows):
        moved = base if at == 0 else pltpu.roll(base, at, 1)
        start = at * per + g * rows
        out[start : start + rows, :] = moved


def flipped(pieces, small):
    return dot(reversing(small), jnp.concatenate(pieces, 1)).astype(BF16)


def diagonal_sum(pairs, g, small, span):
    part = pltpu.roll(
        pairs[g * small : (g + 1) * small, :], 2 * span + 1 - small, 1, stride=1, stride_axis=0
    )
    return jnp.sum(part[:, :span], 0, keepdims=True)


def woven(*jobs):
    live = list(jobs)
    while live:
        for job in list(live):
            if next(job, True):
                live.remove(job)


def own_kernel(span, feat, cot, filt, ks_out, vs_out, z_out, dy_out, qx, kx, vx):
    rows = feat.shape[1]
    width = feat.shape[2]

    def tile(i, carry):
        lanes = pl.ds(pl.multiple_of(i * LANES, LANES), LANES)
        fq, fk, fv = (taps_of(filt, a, lanes) for a in range(3))
        for a, x in enumerate((qx, kx, vx)):
            for at, size in chunks(rows, 32):
                x[at : at + size, :] = feat[a, at : at + size, lanes].astype(F32)
        hole = jnp.zeros((EDGE, LANES), F32)
        for at, size in chunks(rows, 32):
            low = max(at, EDGE)
            c = cot[at : at + size, lanes].astype(F32)[low - at :]
            dy = c * conv(qx, fq, low, at + size - low)
            ks = conv(kx, fk, low, at + size - low)
            vs = conv(vx, fv, low, at + size - low)
            z = ks * vs
            ks_out[low : at + size, lanes] = ks
            vs_out[low : at + size, lanes] = vs
            if at == 0:
                z, dy = (jnp.concatenate([hole, x], 0) for x in (z, dy))
            z_out[at : at + size, lanes] = z.astype(BF16)
            dy_out[at : at + size, lanes] = dy.astype(BF16)
        return carry

    @pl.when(pl.program_id(0) >= 0)
    def _():
        ks_out[0:EDGE, :] = jnp.zeros((EDGE, width), F32)
        vs_out[0:EDGE, :] = jnp.zeros((EDGE, width), F32)

    lax.fori_loop(0, width // LANES, tile, 0)


def column_spec(step, *shape):
    return pl.BlockSpec(shape + (step,), lambda i: (0,) * len(shape) + (i,))


def own_part(features, cotangent, short_filter, span):
    _, rows, width = features.shape
    taps = short_filter.shape[1]
    step = min(width, 512)
    column = functools.partial(column_spec, step)
    kinds = [F32, F32, BF16, BF16]
    return pl.pallas_call(
        functools.partial(own_kernel, span),
        grid=(width // step,),
        in_specs=[column(3, rows), column(rows), column(3, taps)],
        out_specs=[column(rows)] * 4,
        out_shape=[jax.ShapeDtypeStruct((rows, width), kind) for kind in kinds],
        scratch_shapes=[pltpu.VMEM((rows, LANES), F32)] * 3,
        compiler_params=pltpu.CompilerParams(vmem_limit_bytes=67043328),
        cost_estimate=pl.CostEstimate(
            flops=40 * rows * width, bytes_accessed=20 * rows * width, transcendentals=0
        ),
        name="own",
    )(features, cotangent, short_filter)


def join_kernel(
    span, members,
    feat, cot, near, far, filt, lines, ks_in, vs_in, z_in, dy_in,
    grads, keep, send, sums, *scratch,
):
    rows = feat.shape[1]
    width = feat.shape[2]
    per = LANES // members
    blocks = rows // span
    small = span // 2
    wide = rows + EDGE
    odd = odd_place()
    count = len(scratch) // 2
    sets = (scratch[:count], scratch[count:])

    @pl.when(pl.program_id(0) == 0)
    def _():
        for bufs in sets:
            for ref in bufs[3:5]:
                ref[...] = jnp.zeros_like(ref)

    hole = jnp.zeros((EDGE, LANES), F32)

    def halves(low, high):
        return jnp.concatenate([low, high], 0).astype(BF16)

    def column(i):
        return pl.ds(i * LANES, LANES)

    def prepare(i, bufs, state):
        qx, kx, vx, zx, dyx, dqx, dkx, dvx, tst, ust, zm, pairs = bufs
        lanes = column(i)
        fq, fk, fv = (taps_of(filt, a, lanes) for a in range(3))

        def ahead(low, high):
            return jnp.where(odd == 1, near[low:high, lanes], far[low:high, lanes])

        def back(low, high):
            return jnp.where(odd == 1, far[low:high, lanes], near[low:high, lanes])

        ends = ahead(span, span + 4 * EDGE).astype(F32)
        first = back(0, 2 * EDGE).astype(F32)
        last = back(span + EDGE, span + 4 * EDGE).astype(F32)
        nexts = (first[:EDGE], last[:EDGE], last[EDGE : 2 * EDGE])
        c_next = last[2 * EDGE :]
        c_first = cot[0 : 2 * EDGE, lanes].astype(F32)[:EDGE]
        for a, x in enumerate((qx, kx, vx)):
            x[0:EDGE, :] = ends[a * EDGE : (a + 1) * EDGE]
            x[EDGE : 2 * EDGE, :] = feat[a, 0 : 2 * EDGE, lanes].astype(F32)[:EDGE]
            x[2 * EDGE : 3 * EDGE, :] = feat[a, rows - 2 * EDGE : rows, lanes].astype(F32)[EDGE:]
            x[3 * EDGE : 4 * EDGE, :] = nexts[a]
        dy_first = c_first * conv(qx, fq, EDGE, EDGE)
        dy_next = c_next * conv(qx, fq, 3 * EDGE, EDGE)
        ks_first, vs_first = conv(kx, fk, EDGE, EDGE), conv(vx, fv, EDGE, EDGE)
        ks_next, vs_next = conv(kx, fk, 3 * EDGE, EDGE), conv(vx, fv, 3 * EDGE, EDGE)
        top = slice(0, 2 * EDGE)
        dyx[0 : 2 * EDGE, :] = halves(dy_first, dy_in[top, lanes].astype(F32)[EDGE:])
        dyx[2 * EDGE : rows, :] = dy_in[2 * EDGE : rows, lanes]
        dyx[rows : rows + 2 * EDGE, :] = halves(dy_next, first[EDGE:])
        dyx[rows + 2 * EDGE : rows + span + EDGE, :] = back(2 * EDGE, span + EDGE)
        zx[0:span, :] = ahead(0, span)
        z_top = halves(ks_first * vs_first, z_in[top, lanes].astype(F32)[EDGE:])
        zx[span : span + 2 * EDGE, :] = z_top
        zx[span + 2 * EDGE : span + rows, :] = z_in[2 * EDGE : rows, lanes]
        zx[span + rows : span + rows + 2 * EDGE, :] = halves(ks_next * vs_next, hole)

        state[i] = (c_next, ks_first, vs_first, ks_next, vs_next)
        yield False
        filters = lines[i * per : (i + 1) * per, :].astype(BF16)
        turned = dot(filters, reversing(span))
        filters = filters.astype(F32)
        for g in range(per):
            fill_band(ust, g, strip(filters, g, 0), span, per)
            yield False
        for g in range(per):
            fill_band(tst, g, strip(turned, g, 1), span, per)
            yield False

    def multiply(i, bufs, state):
        qx, kx, vx, zx, dyx, dqx, dkx, dvx, tst, ust, zm, pairs = bufs
        lanes = column(i)
        c_next, ks_first, vs_first, ks_next, vs_next = state.pop(i)
        owner = owners(members, blocks)
        one = owners(members, 1)
        rows16 = 2 * EDGE

        def windows(ref):
            return jnp.concatenate([ref[b * span : (b + 2) * span, :] for b in range(blocks)], 1)

        def chunk_of(stacked, at, who):
            start = at * per
            return pick(stacked[start : start + rows16 * per], rows16, who, per)

        dz = dot(ust[...], windows(dyx))
        dz_next = chunk_of(dot(ust[0 : rows16 * per, :], dyx[rows : rows + 2 * span, :]), 0, one)
        dkx[rows:wide, :] = dz_next[:EDGE] * vs_next
        dvx[rows:wide, :] = dz_next[:EDGE] * ks_next
        for at in range(0, span, rows16):
            piece = chunk_of(dz, at, owner)
            for b in range(blocks):
                t = b * span + at
                part = piece[:, b * LANES : (b + 1) * LANES]
                vs, ks = vs_in[t : t + rows16, lanes], ks_in[t : t + rows16, lanes]
                if t == 0:
                    vs = jnp.concatenate([vs_first, vs[EDGE:]], 0)
                    ks = jnp.concatenate([ks_first, ks[EDGE:]], 0)
                dkx[t : t + rows16, :] = part * vs
                dvx[t : t + rows16, :] = part * ks
            yield False
        y = dot(tst[...], windows(zx))
        y_next = chunk_of(dot(tst[0 : rows16 * per, :], zx[rows : rows + 2 * span, :]), 0, one)
        dqx[rows:wide, :] = c_next * y_next[:EDGE]
        starts = range(0, rows, small)
        z_back = flipped([zx[span + t : span + t + small, :] for t in starts], small)
        who = owners(members, len(starts))
        left = list(range(per))

        def mask(g):
            kept = jnp.where(who == g, 1.0, 0.0).astype(BF16)
            zm[g * small : (g + 1) * small, :] = z_back * kept

        for at in range(0, span, rows16):
            piece = chunk_of(y, at, owner)
            for b in range(blocks):
                t = b * span + at
                c = cot[t : t + rows16, lanes].astype(F32)
                dqx[t : t + rows16, :] = c * piece[:, b * LANES : (b + 1) * LANES]
            if left:
                mask(left.pop(0))
            yield False
        for g in left:
            mask(g)
        near_rows = jnp.concatenate([dyx[t : t + 2 * span, :] for t in starts], 1)
        pairs[...] = dot(zm[...], near_rows, ((1,), (1,)))

    def second_stage(i, bufs):
        qx, kx, vx, zx, dyx, dqx, dkx, dvx, tst, ust, zm, pairs = bufs
        lanes = column(i)
        left = list(range(per))

        def diagonal(g):
            sums[1, EDGE + g : EDGE + g + 1, lanes] = diagonal_sum(pairs, g, small, span)

        for a, dx in zip((1, 2, 0), (dkx, dvx, dqx)):
            taps = taps_of(filt, a, lanes)
            parts = [None] * len(taps)
            for at, size in chunks(rows, 32):
                own = feat[a, at : at + size, lanes].astype(F32)
                total = None
                for j, tap in enumerate(taps):
                    moved = dx[pl.ds(at + j, size), :]
                    term = tap * moved
                    total = term if total is None else total + term
                    prod = jnp.sum((own * moved).reshape(size // EDGE, EDGE, LANES), 0)
                    parts[j] = prod if parts[j] is None else parts[j] + prod
                grads[a, at : at + size, lanes] = total.astype(BF16)
                if left:
                    diagonal(left.pop(0))
                yield False
            found = [jnp.sum(p, 0, keepdims=True) for p in parts]
            found.append(jnp.zeros((EDGE - len(taps), LANES), F32))
            sums[a // 2, a % 2 * EDGE : (a % 2 + 1) * EDGE, lanes] = jnp.concatenate(found, 0)
        for g in left:
            diagonal(g)

    tiles = width // LANES
    state = {}
    for i in range(-2, tiles):
        jobs = []
        if i + 2 < tiles:
            jobs.append(prepare(i + 2, sets[i % 2], state))
        if 0 <= i + 1 < tiles:
            jobs.append(multiply(i + 1, sets[(i + 1) % 2], state))
        if i >= 0:
            jobs.append(second_stage(i, sets[i % 2]))
        woven(*jobs)
    keep[...] = sums[odd].astype(BF16)
    send[...] = sums[1 - odd].astype(BF16)


def join(features, cotangent, got, short_filter, long_filter, parts, span, members):
    _, rows, width = features.shape
    taps = short_filter.shape[1]
    step = min(width, 1024)
    per = LANES // members
    wide = rows + EDGE
    tall = rows + 2 * span
    half = (3 * EDGE + per) // 2
    column = functools.partial(column_spec, step)
    buffers = (
        [pltpu.VMEM((4 * EDGE, LANES), F32)] * 3
        + [pltpu.VMEM((tall, LANES), BF16)] * 2
        + [pltpu.VMEM((wide, LANES), F32)] * 3
        + [pltpu.VMEM((per * span, 2 * span), BF16)] * 2
        + [pltpu.VMEM((per * span // 2, 2 * rows // span * LANES), BF16)]
        + [pltpu.VMEM((per * span // 2, 2 * span), F32)]
    )
    return pl.pallas_call(
        functools.partial(join_kernel, span, members),
        grid=(width // step,),
        in_specs=[
            column(3, rows),
            column(rows),
            column(span + 4 * EDGE),
            column(span + 4 * EDGE),
            column(3, taps),
            pl.BlockSpec((step // members, span), lambda i: (i, 0)),
            *[column(rows)] * 4,
        ],
        out_specs=[column(3, rows), column(half), column(half)],
        out_shape=[
            jax.ShapeDtypeStruct((3, rows, width), BF16),
            jax.ShapeDtypeStruct((half, width), BF16),
            jax.ShapeDtypeStruct((half, width), BF16),
        ],
        scratch_shapes=[pltpu.VMEM((2, half, step), F32)] + buffers * 2,
        compiler_params=pltpu.CompilerParams(vmem_limit_bytes=67043328),
        name="join",
    )(features, cotangent, *got, short_filter, long_filter, *parts)


def finish_kernel(count, own, other, *refs):
    *squares, grad_short, grad_long = refs
    odd = odd_place()
    taps = grad_short.shape[1]
    width = own.shape[1]
    per = own.shape[0] - EDGE
    found = [ref[...] for ref in squares]
    while len(found) > 1:
        found = [sum(found[at : at + 2]) for at in range(0, len(found), 2)]
    total = jnp.sum(jnp.sum(found[0], 0, keepdims=True), 1, keepdims=True)
    factor = lax.rsqrt(total / count + 1e-06)

    def put(low, high):
        grad_short[0] = low[0:taps, :] * factor
        grad_short[1] = low[EDGE : EDGE + taps, :] * factor
        grad_short[2] = high[0:taps, :] * factor
        for i in range(width // LANES):
            grad_long[i * per : (i + 1) * per, :] = (
                high[EDGE : EDGE + per, i * LANES : (i + 1) * LANES] * factor
            )

    @pl.when(odd == 0)
    def _():
        put(own, other)

    @pl.when(odd == 1)
    def _():
        put(other, own)


def finish(own, other, squares, taps, groups, span, count):
    width = own.shape[1]
    return pl.pallas_call(
        functools.partial(finish_kernel, count),
        out_shape=[
            jax.ShapeDtypeStruct((3, taps, width), F32),
            jax.ShapeDtypeStruct((groups, span), F32),
        ],
        compiler_params=pltpu.CompilerParams(vmem_limit_bytes=67043328),
        name="finish",
    )(own, other, *squares)


def factors_of(size):
    found = []
    factor = 4
    while size > 1:
        while size % factor == 0:
            found.append(factor)
            size //= factor
        factor = 2 if factor == 4 else factor + 1
    return found


def swap(value, axis, stride, factor, turn):
    route = []
    for i in range(lax.axis_size(axis)):
        digit = i // stride % factor
        other = digit ^ turn if factor in (2, 4) else (digit + turn) % factor
        route.append((i, i + (other - digit) * stride))
    return lax.ppermute(value, axis, route)


def total_over(value, axis, stride, size, kind):
    value = value.astype(F32)
    for factor in factors_of(size):
        sent = value.astype(kind)
        got = [sent] + [swap(sent, axis, stride, factor, turn) for turn in range(1, factor)]
        got = [part.astype(F32) for part in got]
        if factor == 2:
            value = got[0] + got[1]
        elif factor == 4:
            value = (got[0] + got[1]) + (got[2] + got[3])
        else:
            digit = lax.axis_index(axis) // stride % factor
            every = jnp.stack(got[:1] + got[:0:-1])
            ordered = jnp.roll(every, -((factor - digit) % factor), 0)
            value = ordered[0]
            for part in ordered[1:]:
                value = value + part
        stride *= factor
    return value


def on_device(features, short_filter, long_filter, cotangent):
    _, rows, width = features.shape
    taps = short_filter.shape[1]
    groups, span = long_filter.shape
    members = width // groups
    size = lax.axis_size("ctx")
    near, far = edges(features, cotangent, short_filter, span)
    got = (
        lax.ppermute(near, "ctx", [(i, i ^ 1) for i in range(size)]),
        lax.ppermute(far, "ctx", [(i, (i + 1 ^ 1) - 1) for i in range(1, size - 1)]),
    )
    parts = own_part(features, cotangent, short_filter, span)
    grads, keep, send = join(
        features, cotangent, got, short_filter, long_filter, parts, span, members
    )
    own = keep.astype(F32) + swap(send, "ctx", 1, 2, 1).astype(F32)
    own = total_over(own, "ctx", 2, size // 2, BF16)
    other = swap(own, "ctx", 1, 2, 1)
    *early, late = factors_of(lax.axis_size("ch"))
    squares = jnp.sum(own * own + other * other, 0, keepdims=True)
    stride = 1
    for factor in early:
        squares = total_over(squares, "ch", stride, factor, F32)
        stride *= factor
    squares = [squares] + [swap(squares, "ch", stride, late, turn) for turn in range(1, late)]
    count = 3 * taps * D + span * G
    grad_short, grad_long = finish(own, other, squares, taps, groups, span, count)
    return (grads, grad_short, grad_long)


def solution(mesh):
    in_specs = (P(None, "ctx", "ch"), P(None, None, "ch"), P("ch", None), P("ctx", "ch"))
    out_specs = (P(None, "ctx", "ch"), P(None, None, "ch"), P("ch", None))
    return jax.shard_map(
        on_device, mesh=mesh, in_specs=in_specs, out_specs=out_specs, check_vma=False
    )
```

```python
import functools

import jax
import jax.numpy as jnp
from jax import lax
from jax.experimental import pallas as pl
from jax.experimental.pallas import tpu as pltpu
from jax.sharding import PartitionSpec as P

D = 8192
G = 512
LANES = 128
EDGE = 8
F32 = jnp.float32
BF16 = jnp.bfloat16


def taps_of(filt, which, lanes):
    return [filt[which, pl.ds(j, 1), lanes] for j in range(filt.shape[1])]


def conv(source, taps, base, count):
    total = None
    for j, tap in enumerate(taps):
        term = tap * source[pl.ds(base - j, count), :]
        total = term if total is None else total + term
    return total


def chunks(count, size):
    return [(at, min(size, count - at)) for at in range(0, count, size)]


def odd_place():
    return lax.rem(lax.axis_index("ctx"), 2)


def edge_kernel(span, feat, cot, filt, near, far, qx, kx, vx):
    rows = feat.shape[1]
    width = feat.shape[2]
    reach = span + 2 * EDGE

    def run(ahead, back):
        def tile(i, carry):
            lanes = pl.ds(pl.multiple_of(i * LANES, LANES), LANES)
            qx[...] = feat[0, 0:reach, lanes].astype(F32)
            kx[...] = feat[1, rows - reach : rows, lanes].astype(F32)
            vx[...] = feat[2, rows - reach : rows, lanes].astype(F32)
            fq, fk, fv = (taps_of(filt, a, lanes) for a in range(3))
            for at, size in chunks(span, 32):
                z = conv(kx, fk, at + 2 * EDGE, size) * conv(vx, fv, at + 2 * EDGE, size)
                ahead[at : at + size, lanes] = z.astype(BF16)
            q_tail = feat[0, rows - 2 * EDGE : rows, lanes].astype(F32)[EDGE:]
            k_tail = kx[reach - EDGE : reach, :]
            v_tail = vx[reach - EDGE : reach, :]
            tails = jnp.concatenate([q_tail, k_tail, v_tail, v_tail], 0)
            ahead[span : span + 4 * EDGE, lanes] = tails.astype(BF16)
            for at, size in chunks(span + EDGE, 32):
                low = max(at, EDGE)
                c = cot[at : at + max(size, 2 * EDGE), lanes].astype(F32)[low - at : size]
                dy = conv(qx, fq, low, at + size - low) * c
                if at == 0:
                    dy = jnp.concatenate([qx[0:EDGE, :], dy], 0)
                back[at : at + size, lanes] = dy.astype(BF16)
            heads = [feat[a, 0 : 2 * EDGE, lanes].astype(F32)[:EDGE] for a in (1, 2)]
            heads.append(cot[0 : 2 * EDGE, lanes].astype(F32)[:EDGE])
            back[span + EDGE : span + 4 * EDGE, lanes] = jnp.concatenate(heads, 0).astype(BF16)
            return carry

        lax.fori_loop(0, width // LANES, tile, 0)

    odd = odd_place()

    @pl.when(odd == 0)
    def _():
        run(near, far)

    @pl.when(odd == 1)
    def _():
        run(far, near)


def edges(features, cotangent, short_filter, span):
    _, rows, width = features.shape
    taps = short_filter.shape[1]
    step = min(width, 1024)
    return pl.pallas_call(
        functools.partial(edge_kernel, span),
        grid=(width // step,),
        in_specs=[
            pl.BlockSpec((3, rows, step), lambda i: (0, 0, i)),
            pl.BlockSpec((rows, step), lambda i: (0, i)),
            pl.BlockSpec((3, taps, step), lambda i: (0, 0, i)),
        ],
        out_specs=[pl.BlockSpec((span + 4 * EDGE, step), lambda i: (0, i))] * 2,
        out_shape=[jax.ShapeDtypeStruct((span + 4 * EDGE, width), BF16)] * 2,
        scratch_shapes=[pltpu.VMEM((span + 2 * EDGE, LANES), F32)] * 3,
        name="edges",
    )(features, cotangent, short_filter)


def dot(a, b, dims=((1,), (0,))):
    return lax.dot_general(a, b, (dims, ((), ())), preferred_element_type=F32)


def owners(members, count):
    lane = lax.broadcasted_iota(jnp.int32, (1, LANES), 1) // members
    return jnp.concatenate([lane] * count, 1) if count > 1 else lane


def pick(stacked, size, owner, per):
    total = stacked[0:size]
    for g in range(1, per):
        total = jnp.where(owner == g, stacked[g * size : (g + 1) * size], total)
    return total


def strip(filters, g, shift):
    row = filters[g : g + 1, :]
    spread = jnp.concatenate([row, jnp.zeros_like(row)], 1)
    spread = jnp.broadcast_to(spread, (2 * EDGE, spread.shape[1]))
    return pltpu.roll(spread, shift, 1, stride=1, stride_axis=0).astype(BF16)


def reversing(size):
    r = lax.broadcasted_iota(jnp.int32, (size, size), 0)
    s = lax.broadcasted_iota(jnp.int32, (size, size), 1)
    return jnp.where(r + s == size - 1, 1.0, 0.0).astype(BF16)


def fill_band(out, g, base, span, per):
    rows = 2 * EDGE
    for at in range(0, span, rows):
        moved = base if at == 0 else pltpu.roll(base, at, 1)
        start = at * per + g * rows
        out[start : start + rows, :] = moved


def flipped(pieces, small):
    return dot(reversing(small), jnp.concatenate(pieces, 1)).astype(BF16)


def diagonal_sum(pairs, g, small, span):
    part = pltpu.roll(
        pairs[g * small : (g + 1) * small, :], 2 * span + 1 - small, 1, stride=1, stride_axis=0
    )
    return jnp.sum(part[:, :span], 0, keepdims=True)


def woven(*jobs):
    live = list(jobs)
    while live:
        for job in list(live):
            if next(job, True):
                live.remove(job)


def own_kernel(span, feat, cot, filt, ks_out, vs_out, z_out, dy_out, qx, kx, vx):
    rows = feat.shape[1]
    width = feat.shape[2]

    def tile(i, carry):
        lanes = pl.ds(pl.multiple_of(i * LANES, LANES), LANES)
        fq, fk, fv = (taps_of(filt, a, lanes) for a in range(3))
        for a, x in enumerate((qx, kx, vx)):
            for at, size in chunks(rows, 32):
                x[at : at + size, :] = feat[a, at : at + size, lanes].astype(F32)
        hole = jnp.zeros((EDGE, LANES), F32)
        for at, size in chunks(rows, 32):
            low = max(at, EDGE)
            c = cot[at : at + size, lanes].astype(F32)[low - at :]
            dy = c * conv(qx, fq, low, at + size - low)
            ks = conv(kx, fk, low, at + size - low)
            vs = conv(vx, fv, low, at + size - low)
            z = ks * vs
            ks_out[low : at + size, lanes] = ks
            vs_out[low : at + size, lanes] = vs
            if at == 0:
                z, dy = (jnp.concatenate([hole, x], 0) for x in (z, dy))
            z_out[at : at + size, lanes] = z.astype(BF16)
            dy_out[at : at + size, lanes] = dy.astype(BF16)
        return carry

    @pl.when(pl.program_id(0) >= 0)
    def _():
        ks_out[0:EDGE, :] = jnp.zeros((EDGE, width), F32)
        vs_out[0:EDGE, :] = jnp.zeros((EDGE, width), F32)

    lax.fori_loop(0, width // LANES, tile, 0)


def column_spec(step, *shape):
    return pl.BlockSpec(shape + (step,), lambda i: (0,) * len(shape) + (i,))


def own_part(features, cotangent, short_filter, span):
    _, rows, width = features.shape
    taps = short_filter.shape[1]
    step = min(width, 512)
    column = functools.partial(column_spec, step)
    kinds = [F32, F32, BF16, BF16]
    return pl.pallas_call(
        functools.partial(own_kernel, span),
        grid=(width // step,),
        in_specs=[column(3, rows), column(rows), column(3, taps)],
        out_specs=[column(rows)] * 4,
        out_shape=[jax.ShapeDtypeStruct((rows, width), kind) for kind in kinds],
        scratch_shapes=[pltpu.VMEM((rows, LANES), F32)] * 3,
        compiler_params=pltpu.CompilerParams(vmem_limit_bytes=30 * 2**20),
        cost_estimate=pl.CostEstimate(
            flops=40 * rows * width, bytes_accessed=20 * rows * width, transcendentals=0
        ),
        name="own",
    )(*[pltpu.with_memory_space_constraint(x, pltpu.HBM) for x in (features, cotangent, short_filter)])


def join_kernel(
    span, members,
    feat, cot, near, far, filt, lines, ks_in, vs_in, z_in, dy_in,
    grads, keep, send, sums, *scratch,
):
    rows = feat.shape[1]
    width = feat.shape[2]
    per = LANES // members
    blocks = rows // span
    small = span // 2
    wide = rows + EDGE
    odd = odd_place()
    count = len(scratch) // 2
    sets = (scratch[:count], scratch[count:])

    @pl.when(pl.program_id(0) == 0)
    def _():
        for bufs in sets:
            for ref in bufs[3:5]:
                ref[...] = jnp.zeros_like(ref)

    hole = jnp.zeros((EDGE, LANES), F32)

    def halves(low, high):
        return jnp.concatenate([low, high], 0).astype(BF16)

    def column(i):
        return pl.ds(i * LANES, LANES)

    def prepare(i, bufs, state):
        qx, kx, vx, zx, dyx, dqx, dkx, dvx, tst, ust, zm, pairs = bufs
        lanes = column(i)
        fq, fk, fv = (taps_of(filt, a, lanes) for a in range(3))

        def ahead(low, high):
            return jnp.where(odd == 1, near[low:high, lanes], far[low:high, lanes])

        def back(low, high):
            return jnp.where(odd == 1, far[low:high, lanes], near[low:high, lanes])

        ends = ahead(span, span + 4 * EDGE).astype(F32)
        first = back(0, 2 * EDGE).astype(F32)
        last = back(span + EDGE, span + 4 * EDGE).astype(F32)
        nexts = (first[:EDGE], last[:EDGE], last[EDGE : 2 * EDGE])
        c_next = last[2 * EDGE :]
        c_first = cot[0 : 2 * EDGE, lanes].astype(F32)[:EDGE]
        for a, x in enumerate((qx, kx, vx)):
            x[0:EDGE, :] = ends[a * EDGE : (a + 1) * EDGE]
            x[EDGE : 2 * EDGE, :] = feat[a, 0 : 2 * EDGE, lanes].astype(F32)[:EDGE]
            x[2 * EDGE : 3 * EDGE, :] = feat[a, rows - 2 * EDGE : rows, lanes].astype(F32)[EDGE:]
            x[3 * EDGE : 4 * EDGE, :] = nexts[a]
        dy_first = c_first * conv(qx, fq, EDGE, EDGE)
        dy_next = c_next * conv(qx, fq, 3 * EDGE, EDGE)
        ks_first, vs_first = conv(kx, fk, EDGE, EDGE), conv(vx, fv, EDGE, EDGE)
        ks_next, vs_next = conv(kx, fk, 3 * EDGE, EDGE), conv(vx, fv, 3 * EDGE, EDGE)
        top = slice(0, 2 * EDGE)
        dyx[0 : 2 * EDGE, :] = halves(dy_first, dy_in[top, lanes].astype(F32)[EDGE:])
        dyx[2 * EDGE : rows, :] = dy_in[2 * EDGE : rows, lanes]
        dyx[rows : rows + 2 * EDGE, :] = halves(dy_next, first[EDGE:])
        dyx[rows + 2 * EDGE : rows + span + EDGE, :] = back(2 * EDGE, span + EDGE)
        zx[0:span, :] = ahead(0, span)
        z_top = halves(ks_first * vs_first, z_in[top, lanes].astype(F32)[EDGE:])
        zx[span : span + 2 * EDGE, :] = z_top
        zx[span + 2 * EDGE : span + rows, :] = z_in[2 * EDGE : rows, lanes]
        zx[span + rows : span + rows + 2 * EDGE, :] = halves(ks_next * vs_next, hole)

        state[i] = (c_next, ks_first, vs_first, ks_next, vs_next)
        yield False
        filters = lines[i * per : (i + 1) * per, :].astype(BF16)
        turned = dot(filters, reversing(span))
        filters = filters.astype(F32)
        for g in range(per):
            fill_band(ust, g, strip(filters, g, 0), span, per)
            yield False
        for g in range(per):
            fill_band(tst, g, strip(turned, g, 1), span, per)
            yield False

    def multiply(i, bufs, state):
        qx, kx, vx, zx, dyx, dqx, dkx, dvx, tst, ust, zm, pairs = bufs
        lanes = column(i)
        c_next, ks_first, vs_first, ks_next, vs_next = state.pop(i)
        owner = owners(members, blocks)
        one = owners(members, 1)
        rows16 = 2 * EDGE

        def windows(ref):
            return jnp.concatenate([ref[b * span : (b + 2) * span, :] for b in range(blocks)], 1)

        def chunk_of(stacked, at, who):
            start = at * per
            return pick(stacked[start : start + rows16 * per], rows16, who, per)

        dz = dot(ust[...], windows(dyx))
        dz_next = chunk_of(dot(ust[0 : rows16 * per, :], dyx[rows : rows + 2 * span, :]), 0, one)
        dkx[rows:wide, :] = dz_next[:EDGE] * vs_next
        dvx[rows:wide, :] = dz_next[:EDGE] * ks_next
        for at in range(0, span, rows16):
            piece = chunk_of(dz, at, owner)
            for b in range(blocks):
                t = b * span + at
                part = piece[:, b * LANES : (b + 1) * LANES]
                vs, ks = vs_in[t : t + rows16, lanes], ks_in[t : t + rows16, lanes]
                if t == 0:
                    vs = jnp.concatenate([vs_first, vs[EDGE:]], 0)
                    ks = jnp.concatenate([ks_first, ks[EDGE:]], 0)
                dkx[t : t + rows16, :] = part * vs
                dvx[t : t + rows16, :] = part * ks
            yield False
        y = dot(tst[...], windows(zx))
        y_next = chunk_of(dot(tst[0 : rows16 * per, :], zx[rows : rows + 2 * span, :]), 0, one)
        dqx[rows:wide, :] = c_next * y_next[:EDGE]
        starts = range(0, rows, small)
        z_back = flipped([zx[span + t : span + t + small, :] for t in starts], small)
        who = owners(members, len(starts))
        left = list(range(per))

        def mask(g):
            kept = jnp.where(who == g, 1.0, 0.0).astype(BF16)
            zm[g * small : (g + 1) * small, :] = z_back * kept

        for at in range(0, span, rows16):
            piece = chunk_of(y, at, owner)
            for b in range(blocks):
                t = b * span + at
                c = cot[t : t + rows16, lanes].astype(F32)
                dqx[t : t + rows16, :] = c * piece[:, b * LANES : (b + 1) * LANES]
            if left:
                mask(left.pop(0))
            yield False
        for g in left:
            mask(g)
        near_rows = jnp.concatenate([dyx[t : t + 2 * span, :] for t in starts], 1)
        pairs[...] = dot(zm[...], near_rows, ((1,), (1,)))

    def second_stage(i, bufs):
        qx, kx, vx, zx, dyx, dqx, dkx, dvx, tst, ust, zm, pairs = bufs
        lanes = column(i)
        left = list(range(per))

        def diagonal(g):
            sums[1, EDGE + g : EDGE + g + 1, lanes] = diagonal_sum(pairs, g, small, span)

        for a, dx in zip((1, 2, 0), (dkx, dvx, dqx)):
            taps = taps_of(filt, a, lanes)
            parts = [None] * len(taps)
            for at, size in chunks(rows, 32):
                own = feat[a, at : at + size, lanes].astype(F32)
                total = None
                for j, tap in enumerate(taps):
                    moved = dx[pl.ds(at + j, size), :]
                    term = tap * moved
                    total = term if total is None else total + term
                    prod = jnp.sum((own * moved).reshape(size // EDGE, EDGE, LANES), 0)
                    parts[j] = prod if parts[j] is None else parts[j] + prod
                grads[a, at : at + size, lanes] = total.astype(BF16)
                if left:
                    diagonal(left.pop(0))
                yield False
            found = [jnp.sum(p, 0, keepdims=True) for p in parts]
            found.append(jnp.zeros((EDGE - len(taps), LANES), F32))
            sums[a // 2, a % 2 * EDGE : (a % 2 + 1) * EDGE, lanes] = jnp.concatenate(found, 0)
        for g in left:
            diagonal(g)

    tiles = width // LANES
    state = {}
    for i in range(-2, tiles):
        jobs = []
        if i + 2 < tiles:
            jobs.append(prepare(i + 2, sets[i % 2], state))
        if 0 <= i + 1 < tiles:
            jobs.append(multiply(i + 1, sets[(i + 1) % 2], state))
        if i >= 0:
            jobs.append(second_stage(i, sets[i % 2]))
        woven(*jobs)
    keep[...] = sums[odd].astype(BF16)
    send[...] = sums[1 - odd].astype(BF16)


def join(features, cotangent, got, short_filter, long_filter, parts, span, members):
    _, rows, width = features.shape
    taps = short_filter.shape[1]
    step = min(width, 1024)
    per = LANES // members
    wide = rows + EDGE
    tall = rows + 2 * span
    half = (3 * EDGE + per) // 2
    column = functools.partial(column_spec, step)
    buffers = (
        [pltpu.VMEM((4 * EDGE, LANES), F32)] * 3
        + [pltpu.VMEM((tall, LANES), BF16)] * 2
        + [pltpu.VMEM((wide, LANES), F32)] * 3
        + [pltpu.VMEM((per * span, 2 * span), BF16)] * 2
        + [pltpu.VMEM((per * span // 2, 2 * rows // span * LANES), BF16)]
        + [pltpu.VMEM((per * span // 2, 2 * span), F32)]
    )
    return pl.pallas_call(
        functools.partial(join_kernel, span, members),
        grid=(width // step,),
        in_specs=[
            column(3, rows),
            column(rows),
            column(span + 4 * EDGE),
            column(span + 4 * EDGE),
            column(3, taps),
            pl.BlockSpec((step // members, span), lambda i: (i, 0)),
            *[column(rows)] * 4,
        ],
        out_specs=[column(3, rows), column(half), column(half)],
        out_shape=[
            jax.ShapeDtypeStruct((3, rows, width), BF16),
            jax.ShapeDtypeStruct((half, width), BF16),
            jax.ShapeDtypeStruct((half, width), BF16),
        ],
        scratch_shapes=[pltpu.VMEM((2, half, step), F32)] + buffers * 2,
        compiler_params=pltpu.CompilerParams(vmem_limit_bytes=44 * 2**20),
        name="join",
    )(*[pltpu.with_memory_space_constraint(x, pltpu.HBM) for x in (features, cotangent, *got, short_filter, long_filter)], *parts)


def finish_kernel(count, own, other, *refs):
    *squares, grad_short, grad_long = refs
    odd = odd_place()
    taps = grad_short.shape[1]
    width = own.shape[1]
    per = own.shape[0] - EDGE
    found = [ref[...] for ref in squares]
    while len(found) > 1:
        found = [sum(found[at : at + 2]) for at in range(0, len(found), 2)]
    total = jnp.sum(jnp.sum(found[0], 0, keepdims=True), 1, keepdims=True)
    factor = lax.rsqrt(total / count + 1e-06)

    def put(low, high):
        grad_short[0] = low[0:taps, :] * factor
        grad_short[1] = low[EDGE : EDGE + taps, :] * factor
        grad_short[2] = high[0:taps, :] * factor
        for i in range(width // LANES):
            grad_long[i * per : (i + 1) * per, :] = (
                high[EDGE : EDGE + per, i * LANES : (i + 1) * LANES] * factor
            )

    @pl.when(odd == 0)
    def _():
        put(own, other)

    @pl.when(odd == 1)
    def _():
        put(other, own)


def finish(own, other, squares, taps, groups, span, count):
    width = own.shape[1]
    return pl.pallas_call(
        functools.partial(finish_kernel, count),
        out_shape=[
            jax.ShapeDtypeStruct((3, taps, width), F32),
            jax.ShapeDtypeStruct((groups, span), F32),
        ],
        compiler_params=pltpu.CompilerParams(vmem_limit_bytes=67043328),
        name="finish",
    )(*[pltpu.with_memory_space_constraint(x, pltpu.HBM) for x in (own, other, *squares)])


def factors_of(size):
    found = []
    factor = 4
    while size > 1:
        while size % factor == 0:
            found.append(factor)
            size //= factor
        factor = 2 if factor == 4 else factor + 1
    return found


def swap(value, axis, stride, factor, turn):
    route = []
    for i in range(lax.axis_size(axis)):
        digit = i // stride % factor
        other = digit ^ turn if factor in (2, 4) else (digit + turn) % factor
        route.append((i, i + (other - digit) * stride))
    return lax.ppermute(value, axis, route)


def total_over(value, axis, stride, size, kind):
    value = value.astype(F32)
    for factor in factors_of(size):
        sent = value.astype(kind)
        got = [sent] + [swap(sent, axis, stride, factor, turn) for turn in range(1, factor)]
        got = [part.astype(F32) for part in got]
        if factor == 2:
            value = got[0] + got[1]
        elif factor == 4:
            value = (got[0] + got[1]) + (got[2] + got[3])
        else:
            digit = lax.axis_index(axis) // stride % factor
            every = jnp.stack(got[:1] + got[:0:-1])
            ordered = jnp.roll(every, -((factor - digit) % factor), 0)
            value = ordered[0]
            for part in ordered[1:]:
                value = value + part
        stride *= factor
    return value


def on_device(features, short_filter, long_filter, cotangent):
    _, rows, width = features.shape
    taps = short_filter.shape[1]
    groups, span = long_filter.shape
    members = width // groups
    size = lax.axis_size("ctx")
    near, far = edges(features, cotangent, short_filter, span)
    got = (
        lax.ppermute(near, "ctx", [(i, i ^ 1) for i in range(size)]),
        lax.ppermute(far, "ctx", [(i, (i + 1 ^ 1) - 1) for i in range(1, size - 1)]),
    )
    parts = own_part(features, cotangent, short_filter, span)
    grads, keep, send = join(
        features, cotangent, got, short_filter, long_filter, parts, span, members
    )
    own = keep.astype(F32) + swap(send, "ctx", 1, 2, 1).astype(F32)
    own = total_over(own, "ctx", 2, size // 2, BF16)
    other = swap(own, "ctx", 1, 2, 1)
    *early, late = factors_of(lax.axis_size("ch"))
    squares = jnp.sum(own * own + other * other, 0, keepdims=True)
    stride = 1
    for factor in early:
        squares = total_over(squares, "ch", stride, factor, F32)
        stride *= factor
    squares = [squares] + [swap(squares, "ch", stride, late, turn) for turn in range(1, late)]
    count = 3 * taps * D + span * G
    grad_short, grad_long = finish(own, other, squares, taps, groups, span, count)
    return (grads, grad_short, grad_long)


def solution(mesh):
    in_specs = (P(None, "ctx", "ch"), P(None, None, "ch"), P("ch", None), P("ctx", "ch"))
    out_specs = (P(None, "ctx", "ch"), P(None, None, "ch"), P("ch", None))
    return jax.shard_map(
        on_device, mesh=mesh, in_specs=in_specs, out_specs=out_specs, check_vma=False
    )
```

```python
import functools

import jax
import jax.numpy as jnp
from jax import lax
from jax.experimental import pallas as pl
from jax.experimental.pallas import tpu as pltpu
from jax.sharding import PartitionSpec as P


D = 8192
G = 512
LANES = 128
EDGE = 8
F32 = jnp.float32
BF16 = jnp.bfloat16


def taps_of(filt, which, lanes):
    return [filt[which, pl.ds(j, 1), lanes] for j in range(filt.shape[1])]


def conv(source, taps, base, count):
    total = None
    for j, tap in enumerate(taps):
        term = tap * source[pl.ds(base - j, count), :]
        total = term if total is None else total + term
    return total


def chunks(count, size):
    return [(at, min(size, count - at)) for at in range(0, count, size)]


def odd_place():
    return lax.rem(lax.axis_index("ctx"), 2)


def edge_kernel(span, feat, cot, filt, near, far, qx, kx, vx):
    rows = feat.shape[1]
    width = feat.shape[2]
    reach = span + 2 * EDGE

    def run(ahead, back):
        def tile(i, carry):
            lanes = pl.ds(pl.multiple_of(i * LANES, LANES), LANES)
            qx[...] = feat[0, 0:reach, lanes].astype(F32)
            kx[...] = feat[1, rows - reach : rows, lanes].astype(F32)
            vx[...] = feat[2, rows - reach : rows, lanes].astype(F32)
            fq, fk, fv = (taps_of(filt, a, lanes) for a in range(3))
            for at, size in chunks(span, 32):
                z = conv(kx, fk, at + 2 * EDGE, size) * conv(vx, fv, at + 2 * EDGE, size)
                ahead[at : at + size, lanes] = z.astype(BF16)
            q_tail = feat[0, rows - 2 * EDGE : rows, lanes].astype(F32)[EDGE:]
            k_tail = kx[reach - EDGE : reach, :]
            v_tail = vx[reach - EDGE : reach, :]
            tails = jnp.concatenate([q_tail, k_tail, v_tail, v_tail], 0)
            ahead[span : span + 4 * EDGE, lanes] = tails.astype(BF16)
            for at, size in chunks(span + EDGE, 32):
                low = max(at, EDGE)
                c = cot[at : at + max(size, 2 * EDGE), lanes].astype(F32)[low - at : size]
                dy = conv(qx, fq, low, at + size - low) * c
                if at == 0:
                    dy = jnp.concatenate([qx[0:EDGE, :], dy], 0)
                back[at : at + size, lanes] = dy.astype(BF16)
            heads = [feat[a, 0 : 2 * EDGE, lanes].astype(F32)[:EDGE] for a in (1, 2)]
            heads.append(cot[0 : 2 * EDGE, lanes].astype(F32)[:EDGE])
            back[span + EDGE : span + 4 * EDGE, lanes] = jnp.concatenate(heads, 0).astype(BF16)
            return carry

        lax.fori_loop(0, width // LANES, tile, 0)

    odd = odd_place()

    @pl.when(odd == 0)
    def _():
        run(near, far)

    @pl.when(odd == 1)
    def _():
        run(far, near)


def edges(features, cotangent, short_filter, span):
    _, rows, width = features.shape
    taps = short_filter.shape[1]
    step = min(width, 1024)
    return pl.pallas_call(
        functools.partial(edge_kernel, span),
        grid=(width // step,),
        in_specs=[
            pl.BlockSpec((3, rows, step), lambda i: (0, 0, i)),
            pl.BlockSpec((rows, step), lambda i: (0, i)),
            pl.BlockSpec((3, taps, step), lambda i: (0, 0, i)),
        ],
        out_specs=[pl.BlockSpec((span + 4 * EDGE, step), lambda i: (0, i))] * 2,
        out_shape=[jax.ShapeDtypeStruct((span + 4 * EDGE, width), BF16)] * 2,
        scratch_shapes=[pltpu.VMEM((span + 2 * EDGE, LANES), F32)] * 3,
        name="edges",
    )(features, cotangent, short_filter)


def dot(a, b, dims=((1,), (0,))):
    return lax.dot_general(a, b, (dims, ((), ())), preferred_element_type=F32)


def owners(members, count):
    lane = lax.broadcasted_iota(jnp.int32, (1, LANES), 1) // members
    return jnp.concatenate([lane] * count, 1) if count > 1 else lane


def pick(stacked, size, owner, per):
    total = stacked[0:size]
    for g in range(1, per):
        total = jnp.where(owner == g, stacked[g * size : (g + 1) * size], total)
    return total


def strip(filters, g, shift):
    row = filters[g : g + 1, :]
    spread = jnp.concatenate([row, jnp.zeros_like(row)], 1)
    spread = jnp.broadcast_to(spread, (2 * EDGE, spread.shape[1]))
    return pltpu.roll(spread, shift, 1, stride=1, stride_axis=0).astype(BF16)


def reversing(size):
    r = lax.broadcasted_iota(jnp.int32, (size, size), 0)
    s = lax.broadcasted_iota(jnp.int32, (size, size), 1)
    return jnp.where(r + s == size - 1, 1.0, 0.0).astype(BF16)


def fill_band(out, g, base, span, per):
    rows = 2 * EDGE
    for at in range(0, span, rows):
        moved = base if at == 0 else pltpu.roll(base, at, 1)
        start = at * per + g * rows
        out[start : start + rows, :] = moved


def flipped(pieces, small):
    return dot(reversing(small), jnp.concatenate(pieces, 1)).astype(BF16)


def diagonal_sum(pairs, g, small, span):
    part = pltpu.roll(
        pairs[g * small : (g + 1) * small, :], 2 * span + 1 - small, 1, stride=1, stride_axis=0
    )
    return jnp.sum(part[:, :span], 0, keepdims=True)


def woven(*jobs):
    live = list(jobs)
    while live:
        for job in list(live):
            if next(job, True):
                live.remove(job)


def own_kernel(feat, cot, filt, ks_out, vs_out, z_out, dy_out, qx, kx, vx):
    rows = feat.shape[1]
    width = feat.shape[2]

    def tile(i, carry):
        lanes = pl.ds(pl.multiple_of(i * LANES, LANES), LANES)
        fq, fk, fv = (taps_of(filt, a, lanes) for a in range(3))
        for a, x in enumerate((qx, kx, vx)):
            for at, size in chunks(rows, 32):
                x[at : at + size, :] = feat[a, at : at + size, lanes].astype(F32)
        hole = jnp.zeros((EDGE, LANES), F32)
        for at, size in chunks(rows, 32):
            low = max(at, EDGE)
            c = cot[at : at + size, lanes].astype(F32)[low - at :]
            dy = c * conv(qx, fq, low, at + size - low)
            ks = conv(kx, fk, low, at + size - low)
            vs = conv(vx, fv, low, at + size - low)
            z = ks * vs
            ks_out[low : at + size, lanes] = ks
            vs_out[low : at + size, lanes] = vs
            if at == 0:
                z, dy = (jnp.concatenate([hole, x], 0) for x in (z, dy))
            z_out[at : at + size, lanes] = z.astype(BF16)
            dy_out[at : at + size, lanes] = dy.astype(BF16)
        return carry

    @pl.when(pl.program_id(0) >= 0)
    def _():
        ks_out[0:EDGE, :] = jnp.zeros((EDGE, width), F32)
        vs_out[0:EDGE, :] = jnp.zeros((EDGE, width), F32)

    lax.fori_loop(0, width // LANES, tile, 0)


def column_spec(step, *shape):
    return pl.BlockSpec(shape + (step,), lambda i: (0,) * len(shape) + (i,))


def own_part(features, cotangent, short_filter):
    _, rows, width = features.shape
    taps = short_filter.shape[1]
    step = min(width, 512)
    column = functools.partial(column_spec, step)
    kinds = [F32, F32, BF16, BF16]
    return pl.pallas_call(
        own_kernel,
        grid=(width // step,),
        in_specs=[column(3, rows), column(rows), column(3, taps)],
        out_specs=[column(rows)] * 4,
        out_shape=[jax.ShapeDtypeStruct((rows, width), kind) for kind in kinds],
        scratch_shapes=[pltpu.VMEM((rows, LANES), F32)] * 3,
        compiler_params=pltpu.CompilerParams(vmem_limit_bytes=30 * 2**20),
        cost_estimate=pl.CostEstimate(
            flops=40 * rows * width, bytes_accessed=20 * rows * width, transcendentals=0
        ),
        name="own",
    )(*[pltpu.with_memory_space_constraint(x, pltpu.HBM) for x in (features, cotangent, short_filter)])


def join_kernel(
    span, members,
    feat, cot, near, far, filt, lines, ks_in, vs_in, z_in, dy_in,
    grads, keep, send, sums, *scratch,
):
    rows = feat.shape[1]
    width = feat.shape[2]
    per = LANES // members
    blocks = rows // span
    small = span // 2
    wide = rows + EDGE
    odd = odd_place()
    count = len(scratch) // 2
    sets = (scratch[:count], scratch[count:])

    @pl.when(pl.program_id(0) == 0)
    def _():
        for bufs in sets:
            for ref in bufs[3:5]:
                ref[...] = jnp.zeros_like(ref)

    hole = jnp.zeros((EDGE, LANES), F32)

    def halves(low, high):
        return jnp.concatenate([low, high], 0).astype(BF16)

    def column(i):
        return pl.ds(i * LANES, LANES)

    def prepare(i, bufs, state):
        qx, kx, vx, zx, dyx, _, _, _, tst, ust, _, _ = bufs
        lanes = column(i)
        fq, fk, fv = (taps_of(filt, a, lanes) for a in range(3))

        def ahead(low, high):
            return jnp.where(odd == 1, near[low:high, lanes], far[low:high, lanes])

        def back(low, high):
            return jnp.where(odd == 1, far[low:high, lanes], near[low:high, lanes])

        ends = ahead(span, span + 4 * EDGE).astype(F32)
        first = back(0, 2 * EDGE).astype(F32)
        last = back(span + EDGE, span + 4 * EDGE).astype(F32)
        nexts = (first[:EDGE], last[:EDGE], last[EDGE : 2 * EDGE])
        c_next = last[2 * EDGE :]
        c_first = cot[0 : 2 * EDGE, lanes].astype(F32)[:EDGE]
        for a, x in enumerate((qx, kx, vx)):
            x[0:EDGE, :] = ends[a * EDGE : (a + 1) * EDGE]
            x[EDGE : 2 * EDGE, :] = feat[a, 0 : 2 * EDGE, lanes].astype(F32)[:EDGE]
            x[2 * EDGE : 3 * EDGE, :] = feat[a, rows - 2 * EDGE : rows, lanes].astype(F32)[EDGE:]
            x[3 * EDGE : 4 * EDGE, :] = nexts[a]
        dy_first = c_first * conv(qx, fq, EDGE, EDGE)
        dy_next = c_next * conv(qx, fq, 3 * EDGE, EDGE)
        ks_first, vs_first = conv(kx, fk, EDGE, EDGE), conv(vx, fv, EDGE, EDGE)
        ks_next, vs_next = conv(kx, fk, 3 * EDGE, EDGE), conv(vx, fv, 3 * EDGE, EDGE)
        top = slice(0, 2 * EDGE)
        dyx[0 : 2 * EDGE, :] = halves(dy_first, dy_in[top, lanes].astype(F32)[EDGE:])
        dyx[2 * EDGE : rows, :] = dy_in[2 * EDGE : rows, lanes]
        dyx[rows : rows + 2 * EDGE, :] = halves(dy_next, first[EDGE:])
        dyx[rows + 2 * EDGE : rows + span + EDGE, :] = back(2 * EDGE, span + EDGE)
        zx[0:span, :] = ahead(0, span)
        z_top = halves(ks_first * vs_first, z_in[top, lanes].astype(F32)[EDGE:])
        zx[span : span + 2 * EDGE, :] = z_top
        zx[span + 2 * EDGE : span + rows, :] = z_in[2 * EDGE : rows, lanes]
        zx[span + rows : span + rows + 2 * EDGE, :] = halves(ks_next * vs_next, hole)

        state[i] = (c_next, ks_first, vs_first, ks_next, vs_next)
        yield False
        filters = lines[i * per : (i + 1) * per, :].astype(BF16)
        turned = dot(filters, reversing(span))
        filters = filters.astype(F32)
        for g in range(per):
            fill_band(ust, g, strip(filters, g, 0), span, per)
            yield False
        for g in range(per):
            fill_band(tst, g, strip(turned, g, 1), span, per)
            yield False

    def multiply(i, bufs, state):
        _, _, _, zx, dyx, dqx, dkx, dvx, tst, ust, zm, pairs = bufs
        lanes = column(i)
        c_next, ks_first, vs_first, ks_next, vs_next = state.pop(i)
        owner = owners(members, blocks)
        one = owners(members, 1)
        rows16 = 2 * EDGE

        def windows(ref):
            return jnp.concatenate([ref[b * span : (b + 2) * span, :] for b in range(blocks)], 1)

        def chunk_of(stacked, at, who):
            start = at * per
            return pick(stacked[start : start + rows16 * per], rows16, who, per)

        dz = dot(ust[...], windows(dyx))
        dz_next = chunk_of(dot(ust[0 : rows16 * per, :], dyx[rows : rows + 2 * span, :]), 0, one)
        dkx[rows:wide, :] = dz_next[:EDGE] * vs_next
        dvx[rows:wide, :] = dz_next[:EDGE] * ks_next
        for at in range(0, span, rows16):
            piece = chunk_of(dz, at, owner)
            for b in range(blocks):
                t = b * span + at
                part = piece[:, b * LANES : (b + 1) * LANES]
                vs, ks = vs_in[t : t + rows16, lanes], ks_in[t : t + rows16, lanes]
                if t == 0:
                    vs = jnp.concatenate([vs_first, vs[EDGE:]], 0)
                    ks = jnp.concatenate([ks_first, ks[EDGE:]], 0)
                dkx[t : t + rows16, :] = part * vs
                dvx[t : t + rows16, :] = part * ks
            yield False
        y = dot(tst[...], windows(zx))
        y_next = chunk_of(dot(tst[0 : rows16 * per, :], zx[rows : rows + 2 * span, :]), 0, one)
        dqx[rows:wide, :] = c_next * y_next[:EDGE]
        starts = range(0, rows, small)
        z_back = flipped([zx[span + t : span + t + small, :] for t in starts], small)
        who = owners(members, len(starts))
        left = list(range(per))

        def mask(g):
            kept = jnp.where(who == g, 1.0, 0.0).astype(BF16)
            zm[g * small : (g + 1) * small, :] = z_back * kept

        for at in range(0, span, rows16):
            piece = chunk_of(y, at, owner)
            for b in range(blocks):
                t = b * span + at
                c = cot[t : t + rows16, lanes].astype(F32)
                dqx[t : t + rows16, :] = c * piece[:, b * LANES : (b + 1) * LANES]
            if left:
                mask(left.pop(0))
            yield False
        for g in left:
            mask(g)
        near_rows = jnp.concatenate([dyx[t : t + 2 * span, :] for t in starts], 1)
        pairs[...] = dot(zm[...], near_rows, ((1,), (1,)))

    def second_stage(i, bufs):
        _, _, _, _, _, dqx, dkx, dvx, _, _, _, pairs = bufs
        lanes = column(i)
        left = list(range(per))

        def diagonal(g):
            sums[1, EDGE + g : EDGE + g + 1, lanes] = diagonal_sum(pairs, g, small, span)

        for a, dx in zip((1, 2, 0), (dkx, dvx, dqx)):
            taps = taps_of(filt, a, lanes)
            parts = [None] * len(taps)
            for at, size in chunks(rows, 32):
                own = feat[a, at : at + size, lanes].astype(F32)
                total = None
                for j, tap in enumerate(taps):
                    moved = dx[pl.ds(at + j, size), :]
                    term = tap * moved
                    total = term if total is None else total + term
                    prod = jnp.sum((own * moved).reshape(size // EDGE, EDGE, LANES), 0)
                    parts[j] = prod if parts[j] is None else parts[j] + prod
                grads[a, at : at + size, lanes] = total.astype(BF16)
                if left:
                    diagonal(left.pop(0))
                yield False
            found = [jnp.sum(p, 0, keepdims=True) for p in parts]
            found.append(jnp.zeros((EDGE - len(taps), LANES), F32))
            sums[a // 2, a % 2 * EDGE : (a % 2 + 1) * EDGE, lanes] = jnp.concatenate(found, 0)
        for g in left:
            diagonal(g)

    tiles = width // LANES
    state = {}
    for i in range(-2, tiles):
        jobs = []
        if i + 2 < tiles:
            jobs.append(prepare(i + 2, sets[i % 2], state))
        if 0 <= i + 1 < tiles:
            jobs.append(multiply(i + 1, sets[(i + 1) % 2], state))
        if i >= 0:
            jobs.append(second_stage(i, sets[i % 2]))
        woven(*jobs)
    keep[...] = sums[odd].astype(BF16)
    send[...] = sums[1 - odd].astype(BF16)


def join(features, cotangent, got, short_filter, long_filter, parts, span, members):
    _, rows, width = features.shape
    taps = short_filter.shape[1]
    step = min(width, 1024)
    per = LANES // members
    wide = rows + EDGE
    tall = rows + 2 * span
    half = (3 * EDGE + per) // 2
    column = functools.partial(column_spec, step)
    buffers = (
        [pltpu.VMEM((4 * EDGE, LANES), F32)] * 3
        + [pltpu.VMEM((tall, LANES), BF16)] * 2
        + [pltpu.VMEM((wide, LANES), F32)] * 3
        + [pltpu.VMEM((per * span, 2 * span), BF16)] * 2
        + [pltpu.VMEM((per * span // 2, 2 * rows // span * LANES), BF16)]
        + [pltpu.VMEM((per * span // 2, 2 * span), F32)]
    )
    return pl.pallas_call(
        functools.partial(join_kernel, span, members),
        grid=(width // step,),
        in_specs=[
            column(3, rows),
            column(rows),
            column(span + 4 * EDGE),
            column(span + 4 * EDGE),
            column(3, taps),
            pl.BlockSpec((step // members, span), lambda i: (i, 0)),
            *[column(rows)] * 4,
        ],
        out_specs=[column(3, rows), column(half), column(half)],
        out_shape=[
            jax.ShapeDtypeStruct((3, rows, width), BF16),
            jax.ShapeDtypeStruct((half, width), BF16),
            jax.ShapeDtypeStruct((half, width), BF16),
        ],
        scratch_shapes=[pltpu.VMEM((2, half, step), F32)] + buffers * 2,
        compiler_params=pltpu.CompilerParams(vmem_limit_bytes=44 * 2**20),
        name="join",
    )(*[pltpu.with_memory_space_constraint(x, pltpu.HBM) for x in (features, cotangent, *got, short_filter, long_filter)], *parts)


def finish_kernel(count, own, other, *refs):
    *squares, grad_short, grad_long = refs
    odd = odd_place()
    taps = grad_short.shape[1]
    width = own.shape[1]
    per = own.shape[0] - EDGE
    found = [ref[...] for ref in squares]
    while len(found) > 1:
        found = [sum(found[at : at + 2]) for at in range(0, len(found), 2)]
    total = jnp.sum(jnp.sum(found[0], 0, keepdims=True), 1, keepdims=True)
    factor = lax.rsqrt(total / count + 1e-06)

    def put(low, high):
        grad_short[0] = low[0:taps, :] * factor
        grad_short[1] = low[EDGE : EDGE + taps, :] * factor
        grad_short[2] = high[0:taps, :] * factor
        for i in range(width // LANES):
            grad_long[i * per : (i + 1) * per, :] = (
                high[EDGE : EDGE + per, i * LANES : (i + 1) * LANES] * factor
            )

    @pl.when(odd == 0)
    def _():
        put(own, other)

    @pl.when(odd == 1)
    def _():
        put(other, own)


def finish(own, other, squares, taps, groups, span, count):
    width = own.shape[1]
    return pl.pallas_call(
        functools.partial(finish_kernel, count),
        out_shape=[
            jax.ShapeDtypeStruct((3, taps, width), F32),
            jax.ShapeDtypeStruct((groups, span), F32),
        ],
        compiler_params=pltpu.CompilerParams(vmem_limit_bytes=67043328),
        name="finish",
    )(*[pltpu.with_memory_space_constraint(x, pltpu.HBM) for x in (own, other, *squares)])


def factors_of(size):
    found = []
    factor = 4
    while size > 1:
        while size % factor == 0:
            found.append(factor)
            size //= factor
        factor = 2 if factor == 4 else factor + 1
    return found


def swap(value, axis, stride, factor, turn):
    route = []
    for i in range(lax.axis_size(axis)):
        digit = i // stride % factor
        other = digit ^ turn if factor in (2, 4) else (digit + turn) % factor
        route.append((i, i + (other - digit) * stride))
    return lax.ppermute(value, axis, route)


def total_over(value, axis, stride, size, kind):
    value = value.astype(F32)
    for factor in factors_of(size):
        sent = value.astype(kind)
        got = [sent] + [swap(sent, axis, stride, factor, turn) for turn in range(1, factor)]
        got = [part.astype(F32) for part in got]
        if factor == 2:
            value = got[0] + got[1]
        elif factor == 4:
            value = (got[0] + got[1]) + (got[2] + got[3])
        else:
            digit = lax.axis_index(axis) // stride % factor
            every = jnp.stack(got[:1] + got[:0:-1])
            ordered = jnp.roll(every, -((factor - digit) % factor), 0)
            value = ordered[0]
            for part in ordered[1:]:
                value = value + part
        stride *= factor
    return value


def on_device(features, short_filter, long_filter, cotangent):
    _, _, width = features.shape
    taps = short_filter.shape[1]
    groups, span = long_filter.shape
    members = width // groups
    size = lax.axis_size("ctx")
    near, far = edges(features, cotangent, short_filter, span)
    far = lax.ppermute(far, "ctx", [(i, (i + 1 ^ 1) - 1) for i in range(1, size - 1)])
    near = lax.ppermute(near, "ctx", [(i, i ^ 1) for i in range(size)])
    got = (near, far)
    parts = own_part(features, cotangent, short_filter)
    grads, keep, send = join(
        features, cotangent, got, short_filter, long_filter, parts, span, members
    )
    own = keep.astype(F32) + swap(send, "ctx", 1, 2, 1).astype(F32)
    own = total_over(own, "ctx", 2, size // 2, BF16)
    other = swap(own, "ctx", 1, 2, 1)
    *early, late = factors_of(lax.axis_size("ch"))
    squares = jnp.sum(own * own + other * other, 0, keepdims=True)
    stride = 1
    for factor in early:
        squares = total_over(squares, "ch", stride, factor, F32)
        stride *= factor
    squares = [squares] + [swap(squares, "ch", stride, late, turn) for turn in range(1, late)]
    count = 3 * taps * D + span * G
    grad_short, grad_long = finish(own, other, squares, taps, groups, span, count)
    return (grads, grad_short, grad_long)


def solution(mesh):
    in_specs = (P(None, "ctx", "ch"), P(None, None, "ch"), P("ch", None), P("ctx", "ch"))
    out_specs = (P(None, "ctx", "ch"), P(None, None, "ch"), P("ch", None))
    return jax.shard_map(
        on_device, mesh=mesh, in_specs=in_specs, out_specs=out_specs, check_vma=False
    )
```
